256 devices in a mesh: role: 4 (over y), seq: 16 (over x_lo, z), mp: 4 (over x_hi, core).
Axes of the slice: x: 4 (x_hi: 2, x_lo: 2; x = x_hi * 2 + x_lo), y: 4, z: 8, core: 2. Of those that a mesh axis runs over, the one named last changes fastest.
Arguments:
- gen_heads: bfloat16 [1024, 4096], P(None, 'seq'), may hold values from -6 to 6
- gen_resid: bfloat16 [1024, 5120], P('seq', 'mp'), may hold values from -6 to 6
- gen_out_w: bfloat16 [4096, 5120], P('seq', 'mp'), may hold values from -0.09375 to 0.09375
- gen_time_w: bfloat16 [256, 5120], P(None, 'mp'), may hold values from -0.375 to 0.375
- noise: bfloat16 [1024, 5120], P('seq', 'mp'), may hold values from -6 to 6
- steps: int32 [3], replicated, may hold values from 20 to 979
- teacher_qkv: bfloat16 [5120, 3, 4096], P('mp', None, 'seq'), may hold values from -0.078125 to 0.078125
- teacher_out: bfloat16 [4096, 5120], P('seq', 'mp'), may hold values from -0.09375 to 0.09375
- teacher_time: bfloat16 [256, 3, 5120], P(None, None, 'mp'), may hold values from -0.375 to 0.375
- teacher_norm: float32 [2, 4096], P(None, 'seq'), may hold values from 0.5 to 1.5
- critic_qkv: bfloat16 [5120, 3, 4096], P('mp', None, 'seq'), may hold values from -0.078125 to 0.078125
- critic_out: bfloat16 [4096, 5120], P('seq', 'mp'), may hold values from -0.09375 to 0.09375
- critic_time: bfloat16 [256, 3, 5120], P(None, None, 'mp'), may hold values from -0.375 to 0.375
- critic_norm: float32 [2, 4096], P(None, 'seq'), may hold values from 0.5 to 1.5
Outputs:
- latent: bfloat16 [1024, 5120], P('seq', 'mp')
- weight_grad: bfloat16 [4096, 5120], P('seq', 'mp')
The draws below stay inside these ranges and needn't reach their ends.
All inputs are finite; a program needn't handle non-finite values.
Results may differ from the reference program's by a relative error of at most 0.012.
Values may be sent and summed in bfloat16 or wider, within the bound.
A program may use at most 64 MiB of HBM per device.

```python
import math
import jax
import jax.numpy as jnp
from jax import lax

D = 5120
HEAD_DIM = 128
FREQ = 256
HEADS = 32
LENGTH = 1024


def shard_levels(own_key, shape, cuts, low, largest):
    factor_of = 1.0
    for position, parts in cuts:
        heights = jax.random.uniform(jax.random.fold_in(jax.random.fold_in(own_key, 6), position), (parts,), jnp.float32, low / len(cuts), largest / len(cuts))
        factor_of = factor_of * jnp.repeat(jnp.exp(heights), shape[position] // parts).reshape((-1,) + (1,) * (len(shape) - 1 - position))
    return factor_of


def normal_values(rng, dims, spread, most, split=(), held_as=jnp.bfloat16):
    result = spread * jax.random.normal(rng, dims, jnp.float32)
    if split:
        result = result * shard_levels(rng, dims, split, -0.22, 0.18)
    return jnp.clip(result, -most, most).astype(held_as)


def setup_inputs(seed: int = 0) -> dict:
    seeds = jax.random.split(jax.random.key(seed), 15)
    gen_heads = normal_values(seeds[0], (LENGTH, HEADS * HEAD_DIM), 1.0, 6.0, ((1, 16),))
    gen_resid = normal_values(seeds[1], (LENGTH, D), 1.0, 6.0, ((0, 16), (1, 4)))
    gen_out_w = normal_values(seeds[2], (HEADS * HEAD_DIM, D), (HEADS * HEAD_DIM) ** -0.5, 0.09375, ((0, 16), (1, 4)))
    gen_time_w = normal_values(seeds[3], (FREQ, D), FREQ ** -0.5, 0.375, ((1, 4),))
    noise = normal_values(seeds[4], (LENGTH, D), 1.0, 6.0, ((0, 16), (1, 4)))
    steps = jax.random.randint(seeds[5], (3,), 20, 980).astype(jnp.int32)
    teacher_qkv = normal_values(seeds[6], (D, 3, HEADS * HEAD_DIM), D ** -0.5, 0.078125, ((0, 4), (2, 16)))
    teacher_out = normal_values(seeds[7], (HEADS * HEAD_DIM, D), (HEADS * HEAD_DIM) ** -0.5, 0.09375, ((0, 16), (1, 4)))
    teacher_time = normal_values(seeds[8], (FREQ, 3, D), FREQ ** -0.5, 0.375, ((2, 4),))
    teacher_norm = jnp.clip(1.0 + 0.1 * jax.random.normal(seeds[9], (2, HEADS * HEAD_DIM), jnp.float32), 0.5, 1.5)
    critic_qkv = normal_values(seeds[10], (D, 3, HEADS * HEAD_DIM), D ** -0.5, 0.078125, ((0, 4), (2, 16)))
    critic_out = normal_values(seeds[11], (HEADS * HEAD_DIM, D), (HEADS * HEAD_DIM) ** -0.5, 0.09375, ((0, 16), (1, 4)))
    critic_time = normal_values(seeds[12], (FREQ, 3, D), FREQ ** -0.5, 0.375, ((2, 4),))
    critic_norm = jnp.clip(1.0 + 0.1 * jax.random.normal(seeds[13], (2, HEADS * HEAD_DIM), jnp.float32), 0.5, 1.5)
    return {"gen_heads": gen_heads, "gen_resid": gen_resid, "gen_out_w": gen_out_w, "gen_time_w": gen_time_w, "noise": noise, "steps": steps, "teacher_qkv": teacher_qkv, "teacher_out": teacher_out, "teacher_time": teacher_time, "teacher_norm": teacher_norm, "critic_qkv": critic_qkv, "critic_out": critic_out, "critic_time": critic_time, "critic_norm": critic_norm}


def time_embed(step_value):
    half_width = FREQ // 2
    positions = jnp.arange(half_width, dtype=jnp.float32)
    frequencies = jnp.exp(positions * (-math.log(10000.0) / half_width))
    angles = step_value.astype(jnp.float32) * frequencies
    return jnp.concatenate([jnp.cos(angles), jnp.sin(angles)]).astype(jnp.bfloat16)

def head_norm(values, gains):
    factor = lax.rsqrt(lax.optimization_barrier(jnp.mean(values * values, axis=-1, keepdims=True)) + 1e-06)
    return (values * factor * gains).astype(jnp.bfloat16)

def one_head(operands):
    query_head, key_head, value_head = operands
    logits = jnp.dot(query_head, key_head.T, preferred_element_type=jnp.float32) * (1.0 / math.sqrt(HEAD_DIM))
    expanded = jnp.exp(logits)
    probs = (expanded / lax.optimization_barrier(jnp.sum(expanded, axis=1, keepdims=True))).astype(jnp.bfloat16)
    return jnp.dot(probs, value_head, preferred_element_type=jnp.float32).astype(jnp.bfloat16)

def score_pass(latent, noise, level, w_qkv, w_out, w_time, w_norm):
    noise_level = level.astype(jnp.float32) / 1000.0
    noisy = ((1.0 - noise_level) * latent.astype(jnp.float32) + noise_level * noise.astype(jnp.float32)).astype(jnp.bfloat16)
    modulation = jnp.einsum('f,fkd->kd', time_embed(level).astype(jnp.float32), w_time.astype(jnp.float32))
    shift_vec = modulation[0]
    scale_vec = modulation[1]
    gate_vec = modulation[2]
    mean_square = lax.optimization_barrier(jnp.mean(jnp.square(noisy.astype(jnp.float32)), axis=1))
    scaled = (noisy.astype(jnp.float32) * (1.0 + scale_vec)).astype(jnp.bfloat16)
    flat_w = w_qkv.reshape(D, 3 * HEADS * HEAD_DIM)
    projected = jnp.dot(scaled, flat_w, preferred_element_type=jnp.float32)
    shift_proj = jnp.dot(shift_vec.astype(jnp.bfloat16)[None, :], flat_w, preferred_element_type=jnp.float32)[0]
    mixed = projected * lax.rsqrt(mean_square + 1e-06)[:, None] + shift_proj
    mixed = mixed.reshape(LENGTH, 3, HEADS, HEAD_DIM)
    gains = w_norm.reshape(2, HEADS, HEAD_DIM)
    query_norm = head_norm(mixed[:, 0], gains[0])
    key_norm = head_norm(mixed[:, 1], gains[1])
    value_rows = mixed[:, 2].astype(jnp.bfloat16)
    head_out = lax.map(one_head, (query_norm.transpose(1, 0, 2), key_norm.transpose(1, 0, 2), value_rows.transpose(1, 0, 2)))
    head_out = head_out.transpose(1, 0, 2).reshape(LENGTH, HEADS * HEAD_DIM)
    return gate_vec * jnp.dot(head_out, w_out, preferred_element_type=jnp.float32)

def reference(gen_heads, gen_resid, gen_out_w, gen_time_w, noise, steps, teacher_qkv, teacher_out, teacher_time, teacher_norm, critic_qkv, critic_out, critic_time, critic_norm):
    gen_gate = jnp.dot(time_embed(steps[0])[None, :], gen_time_w, preferred_element_type=jnp.float32)[0]
    gen_proj = jnp.dot(gen_heads, gen_out_w, preferred_element_type=jnp.float32)
    latent = (gen_resid.astype(jnp.float32) + gen_gate * gen_proj).astype(jnp.bfloat16)
    total = jnp.zeros((LENGTH, D), jnp.float32)
    for pass_index in range(4):
        level = steps[1 + pass_index // 2]
        if pass_index % 2 == 1:
            predicted = score_pass(latent, noise, level, critic_qkv, critic_out, critic_time, critic_norm)
            total = total + 0.5 * predicted
        else:
            predicted = score_pass(latent, noise, level, teacher_qkv, teacher_out, teacher_time, teacher_norm)
            total = total - 0.5 * predicted
    grad_rows = (gen_gate * total).astype(jnp.bfloat16)
    weight_grad = jnp.dot(gen_heads.T, grad_rows, preferred_element_type=jnp.float32)
    return (latent, weight_grad.astype(jnp.bfloat16))
```

```python
import math

import jax
import jax.numpy as jnp
from jax import lax
from jax.sharding import PartitionSpec as P

D = 5120
HEAD_DIM = 128
BF16 = jnp.bfloat16
F32 = jnp.float32


def time_embed(step_value, width):
    half_width = width // 2
    positions = jnp.arange(half_width, dtype=F32)
    frequencies = jnp.exp(positions * (-math.log(10000.0) / half_width))
    angles = step_value.astype(F32) * frequencies
    return jnp.concatenate([jnp.cos(angles), jnp.sin(angles)]).astype(BF16)


def head_norm(values, gains):
    factor = lax.rsqrt(jnp.mean(values * values, axis=-1, keepdims=True) + 1e-06)
    return (values * factor * gains).astype(BF16)


def dot(a, b):
    return jnp.dot(a, b, preferred_element_type=F32)


def on_device(
    gen_heads,
    gen_resid,
    gen_out_w,
    gen_time_w,
    noise,
    steps,
    teacher_qkv,
    teacher_out,
    teacher_time,
    teacher_norm,
    critic_qkv,
    critic_out,
    critic_time,
    critic_norm,
):
    role = lax.axis_index("role")
    mp = lax.axis_index("mp")
    embeds = jnp.stack([time_embed(steps[i], gen_time_w.shape[0]) for i in range(3)])
    gen_gate = dot(embeds[0:1], gen_time_w)[0]
    modulation = [
        jnp.einsum("lf,fkd->lkd", embeds[1:3], w, preferred_element_type=F32)
        for w in (teacher_time, critic_time)
    ]
    heads_r = lax.dynamic_index_in_dim(
        gen_heads.reshape(16, 4, 16, 256), role, 1, keepdims=False
    ).reshape(256, 256)
    gen_sum = lax.psum_scatter(
        dot(heads_r, gen_out_w).astype(BF16), "seq", scatter_dimension=0, tiled=True
    )
    resid_r = lax.dynamic_slice_in_dim(gen_resid, role * 16, 16, 0)
    noise_r = lax.dynamic_slice_in_dim(noise, role * 16, 16, 0)
    latent_r = (resid_r.astype(F32) + gen_gate * gen_sum.astype(F32)).astype(BF16)
    latent = lax.all_gather(latent_r, "role", axis=0, tiled=True)
    latent_all = lax.all_gather(latent_r, "seq", axis=0, tiled=True)
    noise_all = lax.all_gather(noise_r, "seq", axis=0, tiled=True)
    projected = [None] * 4
    shifts = [None] * 4
    squares = []
    for level in range(2):
        noise_level = steps[1 + level].astype(F32) / 1000.0
        noisy = (
            (1.0 - noise_level) * latent_all.astype(F32) + noise_level * noise_all.astype(F32)
        ).astype(BF16)
        squares.append(jnp.sum(jnp.square(noisy.astype(F32)), axis=1))
        for model, w in enumerate((teacher_qkv, critic_qkv)):
            mod = modulation[model][level]
            scaled = (noisy.astype(F32) * (1.0 + mod[1])).astype(BF16)
            p = 2 * level + model
            projected[p] = jnp.einsum(
                "td,dkc->tkc", scaled, w, preferred_element_type=F32
            ).astype(BF16)
            shifts[p] = jnp.einsum(
                "d,dkc->kc", mod[0].astype(BF16), w, preferred_element_type=F32
            )
    mine = lax.psum_scatter(
        jnp.stack(projected), "mp", scatter_dimension=0, tiled=False
    )
    squares, shifts = lax.psum((jnp.stack(squares), jnp.stack(shifts)), "mp")
    square = lax.dynamic_index_in_dim(squares, mp // 2, 0, keepdims=False)
    shift = lax.dynamic_index_in_dim(shifts, mp, 0, keepdims=False)
    mixed = mine.astype(F32) * lax.rsqrt(square / D + 1e-06)[:, None, None] + shift
    w_norm = jnp.where(mp % 2 == 1, critic_norm, teacher_norm)
    gains = w_norm.reshape(2, 2, HEAD_DIM)
    mixed = mixed.reshape(256, 3, 2, HEAD_DIM)
    query = head_norm(mixed[:, 0], gains[0])
    key = head_norm(mixed[:, 1], gains[1])
    value = mixed[:, 2].astype(BF16)
    kv = lax.all_gather(jnp.stack([key, value]), "role", axis=1, tiled=True)
    logits = jnp.einsum(
        "qhd,khd->hqk", query, kv[0], preferred_element_type=F32
    ) * (1.0 / math.sqrt(HEAD_DIM))
    expanded = jnp.exp(logits)
    probs = (expanded / jnp.sum(expanded, axis=2, keepdims=True)).astype(BF16)
    head_out = jnp.einsum(
        "hqk,khd->qhd", probs, kv[1], preferred_element_type=F32
    ).astype(BF16).reshape(256, 256)
    heads_all = lax.all_gather(head_out, "mp", axis=0, tiled=False)
    score = jnp.zeros((256, 1280), F32)
    for p in range(4):
        gate = modulation[p % 2][p // 2][2]
        out_w = (teacher_out, critic_out)[p % 2]
        score = score + (0.5 if p % 2 else -0.5) * gate * dot(heads_all[p], out_w)
    summed = lax.psum_scatter(score.astype(BF16), "seq", scatter_dimension=0, tiled=True)
    grad_r = (gen_gate * summed.astype(F32)).astype(BF16)
    grad_c = lax.all_to_all(
        grad_r.reshape(16, 4, 320), "role", split_axis=1, concat_axis=0, tiled=False
    ).reshape(64, 320)
    grad_rows = lax.all_gather(grad_c, "seq", axis=0, tiled=True)
    weight_grad = lax.dot_general(
        gen_heads, grad_rows, (((0,), (0,)), ((), ())), preferred_element_type=F32
    ).astype(BF16)
    weight_grad = lax.all_gather(weight_grad, "role", axis=1, tiled=True)
    return (latent, weight_grad)


def solution(mesh):
    in_specs = (
        P(None, "seq"),
        P("seq", "mp"),
        P("seq", "mp"),
        P(None, "mp"),
        P("seq", "mp"),
        P(),
        P("mp", None, "seq"),
        P("seq", "mp"),
        P(None, None, "mp"),
        P(None, "seq"),
        P("mp", None, "seq"),
        P("seq", "mp"),
        P(None, None, "mp"),
        P(None, "seq"),
    )
    out_specs = (P("seq", "mp"), P("seq", "mp"))
    return jax.shard_map(
        on_device, mesh=mesh, in_specs=in_specs, out_specs=out_specs, check_vma=False
    )
```

```python
import math

import jax
import jax.numpy as jnp
from jax import lax
from jax.experimental import pallas as pl
from jax.experimental.pallas import tpu as pltpu
from jax.sharding import PartitionSpec as P

D = 5120
HEAD_DIM = 128
BF16 = jnp.bfloat16
F32 = jnp.float32
MESH = pl.DeviceIdType.MESH
FAR_FIRST = (4, 3, 5, 2, 6, 1, 7)


def time_embed(step_value, width):
    half_width = width // 2
    positions = jnp.arange(half_width, dtype=F32)
    frequencies = jnp.exp(positions * (-math.log(10000.0) / half_width))
    angles = step_value.astype(F32) * frequencies
    return jnp.concatenate([jnp.cos(angles), jnp.sin(angles)]).astype(BF16)


def dot(a, b):
    return jnp.dot(a, b, preferred_element_type=F32)


def dot_t(a, b):
    return lax.dot_general(a, b, (((1,), (1,)), ((), ())), preferred_element_type=F32)


def column_start(role):
    return pl.multiple_of((2 * role + (role + 3) // 4) * 128, 128)


def kernel(
    gh4, resid4, gow, gtw, noise4, emb, lv, tq, cq, tow, cow, ttw, ctw, norms,
    latent_out, grad_out,
    heads_r, heads, ow_gen, tw_gen, resid, wq, ow, tw, nrm, gg, md,
    p1b, p1f, x1r, z1s, z1r, la, na, lat4,
    sc, sqc, sqs, cqr, sqx, xqr,
    cs, cr, of, xs, xr, kvb, qb, hos, ha,
    acc, p2b, x2r, z2s, z2r, grad, ga, wga,
    lsem,
    n_zs, n_zr, n_xs, n_xr,
    a_xs, a_xr, a_zs, a_zr,
    l_zs, l_zr, l_xs, l_xr, l_ys, l_yr,
    b_xs, b_xr, b_zs, b_zr,
    g_ys, g_yr, g_zs, g_zr, g_xs, g_xr,
    m_s, m_r, q_s, q_r, c_s, c_r, x_s, x_r,
    kv_s, kv_r, h_s, h_r, w_s, w_r,
):
    r = lax.axis_index("role")
    s = lax.axis_index("seq")
    m = lax.axis_index("mp")
    xl, z = s // 8, lax.rem(s, 8)
    xh, c = m // 2, lax.rem(m, 2)
    ol = 1 - xl
    oc = 1 - c
    z_of = lambda dz: lax.rem(z + dz, 8)
    z_dev = lambda dz: {"seq": xl * 8 + z_of(dz)}
    x_dev = {"seq": ol * 8 + z}
    core_dev = {"mp": 2 * xh + oc}
    side_dev = lambda level: {"seq": ol * 8 + z, "mp": 2 * level + c}
    y_of = lambda d: lax.rem(r + d, 4)
    y_dev = lambda d: {"role": y_of(d)}

    def rc(src, dst, ssem, rsem, dev):
        return pltpu.make_async_remote_copy(
            src_ref=src, dst_ref=dst, send_sem=ssem, recv_sem=rsem,
            device_id=dev, device_id_type=MESH,
        )

    sent = []

    def send(*args):
        copy = rc(*args)
        copy.start()
        sent.append(copy)

    def got(dst, rsem):
        rc(dst, dst, rsem, rsem, x_dev).wait_recv()

    loads = []

    def load(src, dst):
        copy = pltpu.make_async_copy(src, dst, lsem.at[len(loads)])
        copy.start()
        loads.append(copy)
        return copy

    barrier = pltpu.get_barrier_semaphore()
    peers = [z_dev(dz) for dz in range(1, 8)] + [x_dev, core_dev]
    peers += [side_dev(1 - xh)] + [y_dev(d) for d in (1, 2, 3)]
    for dev in peers:
        pl.semaphore_signal(barrier, inc=1, device_id=dev, device_id_type=MESH)
    l_heads = load(gh4.at[:, r], heads_r)
    l_gow = load(gow, ow_gen)
    l_noise = load(noise4.at[r], na.at[s])
    l_resid = load(resid4.at[r], resid)
    l_gtw = load(gtw, tw_gen)
    l_tt = load(ttw, tw.at[0])
    l_ct = load(ctw, tw.at[1])
    l_tq = load(tq, wq.at[0])
    l_cq = load(cq, wq.at[1])
    l_to = load(tow, ow.at[0])
    l_co = load(cow, ow.at[1])
    l_all = load(gh4, heads)
    l_heads.wait()
    l_gow.wait()
    l_noise.wait()
    part = dot(heads_r[pl.ds(ol * 8, 8)].reshape(128, 256), ow_gen[...])
    p1b[...] = part.astype(BF16).reshape(8, 16, 1280)
    pl.semaphore_wait(barrier, len(peers))

    for dz in FAR_FIRST:
        send(na.at[s], na.at[s], n_zs.at[dz], n_zr.at[z], z_dev(dz))
    send(norms, nrm, m_s, m_r, x_dev)

    def sum_start(pb, xr_buf, xs_sem, xr_sem):
        for dz in FAR_FIRST + (0,):
            zz = z_of(dz)
            send(pb.at[zz], xr_buf.at[zz], xs_sem.at[zz], xr_sem.at[zz], x_dev)

    def sum_middle(pf, xr_buf, xr_sem, zs_buf, zr_buf, zs_sem, zr_sem):
        for dz in FAR_FIRST:
            zz = z_of(dz)
            got(xr_buf.at[zz], xr_sem.at[zz])
            zs_buf[zz] = (pf[zz] + xr_buf[zz].astype(F32)).astype(BF16)
            send(zs_buf.at[zz], zr_buf.at[z], zs_sem.at[dz], zr_sem.at[z], z_dev(dz))

    def sum_end(pf, xr_buf, xr_sem, zr_buf, zr_sem):
        got(xr_buf.at[z], xr_sem.at[z])
        total = pf[z] + xr_buf[z].astype(F32)
        for dz in reversed(FAR_FIRST):
            zz = z_of(dz)
            got(zr_buf.at[zz], zr_sem.at[zz])
            total = total + zr_buf[zz].astype(F32)
        return total

    sum_start(p1b, x1r, a_xs, a_xr)
    p1f[...] = dot(heads_r[pl.ds(xl * 8, 8)].reshape(128, 256), ow_gen[...]).reshape(8, 16, 1280)
    sum_middle(p1f, x1r, a_xr, z1s, z1r, a_zs, a_zr)
    send(na.at[s], na.at[s], n_xs.at[z], n_xr.at[z], x_dev)
    for dz in reversed(FAR_FIRST):
        zz = z_of(dz)
        got(na.at[xl * 8 + zz], n_zr.at[zz])
        send(na.at[xl * 8 + zz], na.at[xl * 8 + zz], n_xs.at[zz], n_xr.at[zz], x_dev)

    l_gtw.wait()
    gg[...] = dot(emb[...], tw_gen[...])
    l_tt.wait()
    l_ct.wait()

    def modulate(i, carry):
        md[i // 3, lax.rem(i, 3)] = dot(emb[...], tw[i // 3, lax.rem(i, 3)])
        return carry

    lax.fori_loop(0, 6, modulate, 0)
    l_resid.wait()

    total = sum_end(p1f, x1r, a_xr, z1r, a_zr)
    latent = (resid[...].astype(F32) + gg[0:1, :] * total).astype(BF16)
    la[s] = latent
    lat4[r] = latent

    for dz in FAR_FIRST:
        send(la.at[s], la.at[s], l_zs.at[dz], l_zr.at[z], z_dev(dz))
    send(la.at[s], la.at[s], l_xs.at[z], l_xr.at[z], x_dev)
    for d in (1, 2, 3):
        send(lat4.at[r], lat4.at[r], l_ys.at[d], l_yr.at[r], y_dev(d))
    for level in range(2):
        for model in range(2):
            first = lax.broadcasted_iota(jnp.int32, (16, 1280), 0) == 0
            shift = md[model, 0, 1 + level : 2 + level, :]
            sc[level, model, 256:272, :] = jnp.where(first, shift, 0.0).astype(BF16)

    def prepare(b):
        rows = pl.ds(pl.multiple_of(b * 16, 16), 16)
        lat = la[b].astype(F32)
        noi = na[b].astype(F32)
        for level in range(2):
            sl = lv[level : level + 1, 0:1]
            noisy = ((1.0 - sl) * lat + sl * noi).astype(BF16).astype(F32)
            square = jnp.sum(noisy * noisy, axis=1, keepdims=True)
            sqc[level, rows, :] = jnp.broadcast_to(square, (16, 128))
            for model in range(2):
                scale = 1.0 + md[model, 1, 1 + level : 2 + level, :]
                sc[level, model, rows, :] = (noisy * scale).astype(BF16)

    prepare(s)
    for dz in reversed(FAR_FIRST):
        zz = z_of(dz)
        b = xl * 8 + zz
        got(la.at[b], l_zr.at[zz])
        send(la.at[b], la.at[b], l_xs.at[zz], l_xr.at[zz], x_dev)
        prepare(b)
    for dz in (0,) + tuple(reversed(FAR_FIRST)):
        zz = z_of(dz)
        b = ol * 8 + zz
        got(la.at[b], l_xr.at[zz])
        got(na.at[b], n_xr.at[zz])
        prepare(b)

    l_tq.wait()
    l_cq.wait()

    def qkv_dots(k):
        kind = (k + 1) % 3
        for level in range(2):
            cs[k, level] = dot(sc[level, oc], wq[oc, kind]).astype(BF16)
            send(cs.at[k, level], cr.at[k, level], c_s.at[k, level], c_r.at[k, level], core_dev)
        for level in range(2):
            of[k % 2, level] = dot(sc[level, c], wq[c, kind])

    def qkv_sums(k):
        for level in range(2):
            got(cr.at[k, level], c_r.at[k, level])
            xs[k, level] = (of[k % 2, level] + cr[k, level].astype(F32)).astype(BF16)
            send(xs.at[k, level], xr.at[k, xh], x_s.at[k, level], x_r.at[k, xh], side_dev(level))

    for level in range(2):
        row = jnp.transpose(sqc[level])[0:8, :]
        sqs[level] = row
    send(sqs, cqr, q_s.at[0], q_r.at[0], core_dev)
    qkv_dots(0)
    got(cqr, q_r.at[0])
    sqx[...] = sqs[...] + cqr[...]
    for level in range(2):
        send(sqx.at[level], xqr.at[xh], q_s.at[1 + level], q_r.at[1 + xh], side_dev(level))
    qkv_dots(1)
    qkv_sums(0)
    qkv_dots(2)
    qkv_sums(1)
    qkv_sums(2)

    for i in range(2):
        got(xqr.at[i], q_r.at[1 + i])
    square = jnp.broadcast_to((xqr[0] + xqr[1])[0:1, :], (128, 256))
    rinv = lax.rsqrt(jnp.transpose(square) * (1.0 / D) + 1e-06)
    got(nrm, m_r)

    def mixed_head(k, h):
        cols = slice(h * 128, h * 128 + 128)
        both = xr[k, 0, :, cols].astype(F32) + xr[k, 1, :, cols].astype(F32)
        return both[0:256] * rinv + both[256:257]

    def normed(values, gains):
        factor = lax.rsqrt(jnp.mean(values * values, axis=-1, keepdims=True) + 1e-06)
        return (values * factor * gains).astype(BF16)

    for k in range(2):
        for i in range(2):
            got(xr.at[k, i], x_r.at[k, i])
        for h in range(2):
            cols = slice(h * 128, h * 128 + 128)
            values = mixed_head(k, h)
            if k == 0:
                values = normed(values, nrm[c, 1:2, cols])
            kvb[k, r, :, cols] = values.astype(BF16)
        for d in (1, 3):
            send(kvb.at[k, r], kvb.at[k, r], kv_s.at[k, d], kv_r.at[k, r], y_dev(d))
    for i in range(2):
        got(xr.at[2, i], x_r.at[2, i])
    for h in range(2):
        cols = slice(h * 128, h * 128 + 128)
        qb[h] = normed(mixed_head(2, h), nrm[c, 0:1, cols])
    below, above, across = y_of(3), y_of(1), y_of(2)
    got(kvb.at[0, below], kv_r.at[0, below])
    send(kvb.at[0, below], kvb.at[0, below], kv_s.at[0, 2], kv_r.at[0, below], y_dev(1))
    got(kvb.at[0, above], kv_r.at[0, above])
    got(kvb.at[1, above], kv_r.at[1, above])
    send(kvb.at[1, above], kvb.at[1, above], kv_s.at[1, 2], kv_r.at[1, above], y_dev(3))

    exponent = math.log2(math.e) / math.sqrt(HEAD_DIM)
    sums = [jnp.zeros((256, 1), F32)] * 2
    outs = [jnp.zeros((256, 128), F32)] * 2
    for n, b in enumerate((r, above, below, across)):
        if n == 2:
            got(kvb.at[1, below], kv_r.at[1, below])
        if n == 3:
            got(kvb.at[0, across], kv_r.at[0, across])
            got(kvb.at[1, across], kv_r.at[1, across])
        for h in range(2):
            cols = slice(h * 128, h * 128 + 128)
            e = jnp.exp2(dot_t(qb[h], kvb[0, b, :, cols]) * exponent)
            sums[h] = sums[h] + jnp.sum(e, axis=1, keepdims=True)
            outs[h] = outs[h] + dot(e.astype(BF16), kvb[1, b, :, cols])
    for h in range(2):
        hos[:, h * 128 : h * 128 + 128] = (outs[h] / sums[h]).astype(BF16)
    for level in range(2):
        send(hos, ha.at[xh, c], h_s.at[level], h_r.at[xh, c], side_dev(level))

    l_to.wait()
    l_co.wait()

    def out_term(level, model, half):
        sign = (model.astype(F32) - 0.5) * md[model, 2, 1 + level : 2 + level, :]
        return sign * dot(ha[level, model, pl.ds(pl.multiple_of(half * 128, 128), 128)], ow[model])

    for level in range(2):
        got(ha.at[level, c], h_r.at[level, c])
        send(ha.at[level, c], ha.at[level, c], h_s.at[2 + level], h_r.at[level, c], core_dev)
    for half in range(2):
        acc[half] = out_term(0, c, half) + out_term(1, c, half)
    for level in range(2):
        got(ha.at[level, oc], h_r.at[level, oc])
    p2b[...] = (acc[ol] + out_term(0, oc, ol) + out_term(1, oc, ol)).astype(BF16).reshape(8, 16, 1280)
    sum_start(p2b, x2r, b_xs, b_xr)
    p1f[...] = (acc[xl] + out_term(0, oc, xl) + out_term(1, oc, xl)).reshape(8, 16, 1280)
    sum_middle(p1f, x2r, b_xr, z2s, z2r, b_zs, b_zr)
    for d in (1, 2, 3):
        got(lat4.at[y_of(d)], l_yr.at[y_of(d)])
    latent_out[...] = lat4[...].reshape(64, 1280)
    total = sum_end(p1f, x2r, b_xr, z2r, b_zr)
    grad[...] = (gg[0:1, :] * total).astype(BF16)

    for d in (2, 1, 3):
        src = grad.at[:, pl.ds(column_start(y_of(d)), 384)]
        send(src, ga.at[s, r], g_ys.at[d], g_yr.at[r], y_dev(d))
    ga[s, r] = grad[:, pl.ds(column_start(r), 384)]
    for d in (1, 3, 2):
        got(ga.at[s, y_of(d)], g_yr.at[y_of(d)])
    for dz in FAR_FIRST:
        send(ga.at[s], ga.at[s], g_zs.at[dz], g_zr.at[z], z_dev(dz))
    send(ga.at[s], ga.at[s], g_xs.at[z], g_xr.at[z], x_dev)
    for dz in reversed(FAR_FIRST):
        zz = z_of(dz)
        b = xl * 8 + zz
        got(ga.at[b], g_zr.at[zz])
        send(ga.at[b], ga.at[b], g_xs.at[zz], g_xr.at[zz], x_dev)
    l_all.wait()

    def grad_term(half):
        lhs = heads[pl.ds(half * 8, 8)].reshape(512, 256)
        rhs = ga[pl.ds(half * 8, 8)].reshape(512, 384)
        return lax.dot_general(lhs, rhs, (((0,), (0,)), ((), ())), preferred_element_type=F32)

    first_half = grad_term(xl)
    for dz in range(8):
        zz = z_of(dz)
        got(ga.at[ol * 8 + zz], g_xr.at[zz])
    wga[r] = (first_half + grad_term(ol)).astype(BF16).reshape(2, 128, 384)
    for i, d in ((0, 1), (1, 3), (1, 1), (0, 3)):
        send(wga.at[r, i], wga.at[r, i], w_s.at[i, d], w_r.at[i, r], y_dev(d))
    got(wga.at[below, 0], w_r.at[0, below])
    send(wga.at[below, 0], wga.at[below, 0], w_s.at[0, 2], w_r.at[0, below], y_dev(1))
    got(wga.at[above, 1], w_r.at[1, above])
    send(wga.at[above, 1], wga.at[above, 1], w_s.at[1, 2], w_r.at[1, above], y_dev(3))
    got(wga.at[below, 1], w_r.at[1, below])
    got(wga.at[above, 0], w_r.at[0, above])
    got(wga.at[across, 0], w_r.at[0, across])
    got(wga.at[across, 1], w_r.at[1, across])
    for i in range(2):
        rows = slice(i * 128, i * 128 + 128)
        grad_out[rows, 0:384] = wga[0, i]
        grad_out[rows, 384:768] = wga[1, i]
        grad_out[rows, 768:1024] = wga[2, i, :, 128:384]
        grad_out[rows, 1024:1280] = wga[3, i, :, 128:384]
    for copy in sent:
        copy.wait_send()


def on_device(
    gen_heads,
    gen_resid,
    gen_out_w,
    gen_time_w,
    noise,
    steps,
    teacher_qkv,
    teacher_out,
    teacher_time,
    teacher_norm,
    critic_qkv,
    critic_out,
    critic_time,
    critic_norm,
):
    embeds = jnp.stack([time_embed(steps[min(i, 2)], gen_time_w.shape[0]) for i in range(8)])
    levels = jnp.broadcast_to(
        jnp.pad(steps[1:3].astype(F32) / 1000.0, (0, 6))[:, None], (8, 128)
    )
    norms = jnp.stack([teacher_norm, critic_norm])
    vmem = pl.BlockSpec(memory_space=pltpu.VMEM)
    hbm = pl.BlockSpec(memory_space=pl.ANY)
    V = pltpu.VMEM
    S = pltpu.SemaphoreType.DMA
    block = (16, 1280)
    scratch = [
        V((16, 16, 256), BF16), V((16, 4, 16, 256), BF16), V((256, 1280), BF16),
        V((256, 1280), BF16), V(block, BF16), V((2, 3, 1280, 256), BF16),
        V((2, 256, 1280), BF16), V((2, 3, 256, 1280), BF16), V((2, 2, 256), F32),
        V((8, 1280), F32), V((2, 3, 8, 1280), F32),
        V((8,) + block, BF16), V((8,) + block, F32), V((8,) + block, BF16),
        V((8,) + block, BF16), V((8,) + block, BF16),
        V((16,) + block, BF16), V((16,) + block, BF16), V((4,) + block, BF16),
        V((2, 2, 272, 1280), BF16), V((2, 256, 128), F32),
        V((2, 8, 256), F32), V((2, 8, 256), F32), V((2, 8, 256), F32), V((2, 8, 256), F32),
        V((3, 2, 272, 256), BF16), V((3, 2, 272, 256), BF16), V((2, 2, 272, 256), F32),
        V((3, 2, 272, 256), BF16), V((3, 2, 272, 256), BF16),
        V((2, 4, 256, 256), BF16), V((2, 256, 128), BF16), V((256, 256), BF16),
        V((2, 2, 256, 256), BF16),
        V((2, 128, 1280), F32), V((8,) + block, BF16), V((8,) + block, BF16),
        V((8,) + block, BF16), V((8,) + block, BF16),
        V(block, BF16), V((16, 4, 16, 384), BF16), V((4, 2, 128, 384), BF16),
        S((12,)),
        S((8,)), S((8,)), S((8,)), S((8,)),
        S((8,)), S((8,)), S((8,)), S((8,)),
        S((8,)), S((8,)), S((8,)), S((8,)), S((4,)), S((4,)),
        S((8,)), S((8,)), S((8,)), S((8,)),
        S((4,)), S((4,)), S((8,)), S((8,)), S((8,)), S((8,)),
        S(()), S(()), S((3,)), S((3,)), S((3, 2)), S((3, 2)), S((3, 2)), S((3, 2)),
        S((2, 4)), S((2, 4)), S((4,)), S((2, 2)), S((2, 4)), S((2, 4)),
    ]
    latent, weight_grad = pl.pallas_call(
        kernel,
        out_shape=(
            jax.ShapeDtypeStruct((64, 1280), BF16),
            jax.ShapeDtypeStruct((256, 1280), BF16),
        ),
        in_specs=[hbm] * 5 + [vmem] * 2 + [hbm] * 6 + [vmem],
        out_specs=(vmem, vmem),
        scratch_shapes=scratch,
        compiler_params=pltpu.CompilerParams(
            collective_id=0, has_side_effects=True, vmem_limit_bytes=60 * 1024 * 1024
        ),
        name="step",
    )(
        gen_heads.reshape(16, 4, 16, 256),
        gen_resid.reshape(4, 16, 1280),
        gen_out_w,
        gen_time_w,
        noise.reshape(4, 16, 1280),
        embeds,
        levels,
        teacher_qkv.transpose(1, 0, 2),
        critic_qkv.transpose(1, 0, 2),
        teacher_out,
        critic_out,
        teacher_time.transpose(1, 0, 2),
        critic_time.transpose(1, 0, 2),
        norms,
    )
    return (latent, weight_grad)


def solution(mesh):
    in_specs = (
        P(None, "seq"),
        P("seq", "mp"),
        P("seq", "mp"),
        P(None, "mp"),
        P("seq", "mp"),
        P(),
        P("mp", None, "seq"),
        P("seq", "mp"),
        P(None, None, "mp"),
        P(None, "seq"),
        P("mp", None, "seq"),
        P("seq", "mp"),
        P(None, None, "mp"),
        P(None, "seq"),
    )
    out_specs = (P("seq", "mp"), P("seq", "mp"))
    return jax.shard_map(
        on_device, mesh=mesh, in_specs=in_specs, out_specs=out_specs, check_vma=False
    )
```

```python
import math

import jax
import jax.numpy as jnp
from jax import lax
from jax.experimental import pallas as pl
from jax.experimental.pallas import tpu as pltpu
from jax.sharding import PartitionSpec as P

D = 5120
HEAD_DIM = 128
BF16 = jnp.bfloat16
F32 = jnp.float32
MESH = pl.DeviceIdType.MESH
FAR_FIRST = (4, 3, 5, 2, 6, 1, 7)
NEAR_FIRST = (1, 7, 2, 6, 3, 5, 4)


def time_embeds(steps):
    row = lax.broadcasted_iota(jnp.int32, (8, 128), 0)
    values = jnp.where(row == 0, steps[0], jnp.where(row == 1, steps[1], steps[2])).astype(F32)
    positions = lax.broadcasted_iota(jnp.int32, (8, 128), 1).astype(F32)
    angles = values * jnp.exp(positions * (-math.log(10000.0) / 128))
    return jnp.concatenate([jnp.cos(angles), jnp.sin(angles)], axis=1).astype(BF16), values


def dot(a, b):
    return jnp.dot(a, b, preferred_element_type=F32)


def dot_t(a, b):
    return lax.dot_general(a, b, (((1,), (1,)), ((), ())), preferred_element_type=F32)


def column_start(role):
    return pl.multiple_of((2 * role + (role + 3) // 4) * 128, 128)


def kernel(
    gh4, resid4, gow, gtw, noise4, steps, tq, cq, tow, cow, ttw, ctw, t_norm, c_norm,
    latent_out, grad_out,
    heads_r, heads, ow_gen, tw_gen, resid, wq, ow, tw, nrm, gg, md,
    p1b, p1f, x1r, z1s, z1r, la, na, lat4,
    sc, sqc, sqs, cqr, sqx, xqr,
    cs, cr, of, xs, xr, kvb, qb, hos, ha,
    acc, p2b, x2r, z2s, z2r, grad, ga, wga,
    lsem,
    n_zs, n_zr, n_xs, n_xr,
    a_xs, a_xr, a_zs, a_zr,
    l_zs, l_zr, l_xs, l_xr, l_ys, l_yr,
    b_xs, b_xr, b_zs, b_zr,
    g_ys, g_yr, g_zs, g_zr, g_xs, g_xr,
    m_s, m_r, q_s, q_r, c_s, c_r, x_s, x_r,
    kv_s, kv_r, h_s, h_r, w_s, w_r,
):
    r = lax.axis_index("role")
    s = lax.axis_index("seq")
    m = lax.axis_index("mp")
    xl, z = s // 8, lax.rem(s, 8)
    xh, c = m // 2, lax.rem(m, 2)
    ol = 1 - xl
    oc = 1 - c
    z_of = lambda dz: lax.rem(z + dz, 8)
    z_dev = lambda dz: {"seq": xl * 8 + z_of(dz)}
    x_dev = {"seq": ol * 8 + z}
    core_dev = {"mp": 2 * xh + oc}
    side_dev = lambda level: {"seq": ol * 8 + z, "mp": 2 * level + c}
    y_of = lambda d: lax.rem(r + d, 4)
    y_dev = lambda d: {"role": y_of(d)}

    def rc(src, dst, ssem, rsem, dev):
        return pltpu.make_async_remote_copy(
            src_ref=src, dst_ref=dst, send_sem=ssem, recv_sem=rsem,
            device_id=dev, device_id_type=MESH,
        )

    sent = []

    def send(*args):
        copy = rc(*args)
        copy.start()
        sent.append(copy)

    def got(dst, rsem):
        rc(dst, dst, rsem, rsem, x_dev).wait_recv()

    loads = []

    def load(src, dst):
        copy = pltpu.make_async_copy(src, dst, lsem.at[len(loads)])
        copy.start()
        loads.append(copy)
        return copy

    barrier = pltpu.get_barrier_semaphore()
    peers = [z_dev(dz) for dz in range(1, 8)] + [x_dev, core_dev]
    peers += [side_dev(1 - xh)] + [y_dev(d) for d in (1, 2, 3)]
    for dev in peers:
        pl.semaphore_signal(barrier, inc=1, device_id=dev, device_id_type=MESH)
    l_heads = load(gh4.at[:, r], heads_r)
    l_gow = load(gow, ow_gen)
    l_noise = load(noise4.at[r], na.at[s])
    l_resid = load(resid4.at[r], resid)
    l_gtw = load(gtw, tw_gen)
    l_tt = load(ttw, tw.at[0])
    l_ct = load(ctw, tw.at[1])
    l_tq = load(tq, wq.at[0])
    l_cq = load(cq, wq.at[1])
    l_to = load(tow, ow.at[0])
    l_co = load(cow, ow.at[1])
    l_all = load(gh4, heads)
    l_heads.wait()
    l_gow.wait()
    l_noise.wait()
    part = dot(heads_r[pl.ds(ol * 8, 8)].reshape(128, 256), ow_gen[...])
    p1b[...] = part.astype(BF16).reshape(8, 16, 1280)
    pl.semaphore_wait(barrier, len(peers))

    for dz in NEAR_FIRST:
        send(na.at[s], na.at[s], n_zs.at[dz], n_zr.at[z], z_dev(dz))
    for i, norm in enumerate((t_norm, c_norm)):
        send(norm, nrm.at[i], m_s.at[i], m_r.at[i], x_dev)

    def sum_start(pb, xr_buf, xs_sem, xr_sem):
        for dz in FAR_FIRST + (0,):
            zz = z_of(dz)
            send(pb.at[zz], xr_buf.at[zz], xs_sem.at[zz], xr_sem.at[zz], x_dev)

    def sum_middle(pf, xr_buf, xr_sem, zs_buf, zr_buf, zs_sem, zr_sem):
        for dz in FAR_FIRST:
            zz = z_of(dz)
            got(xr_buf.at[zz], xr_sem.at[zz])
            zs_buf[zz] = (pf[zz] + xr_buf[zz].astype(F32)).astype(BF16)
            send(zs_buf.at[zz], zr_buf.at[z], zs_sem.at[dz], zr_sem.at[z], z_dev(dz))

    def sum_end(pf, xr_buf, xr_sem, zr_buf, zr_sem):
        got(xr_buf.at[z], xr_sem.at[z])
        total = pf[z] + xr_buf[z].astype(F32)
        for dz in NEAR_FIRST:
            zz = z_of(dz)
            got(zr_buf.at[zz], zr_sem.at[zz])
            total = total + zr_buf[zz].astype(F32)
        return total

    sum_start(p1b, x1r, a_xs, a_xr)
    p1f[...] = dot(heads_r[pl.ds(xl * 8, 8)].reshape(128, 256), ow_gen[...]).reshape(8, 16, 1280)
    sum_middle(p1f, x1r, a_xr, z1s, z1r, a_zs, a_zr)
    send(na.at[s], na.at[s], n_xs.at[z], n_xr.at[z], x_dev)
    for dz in NEAR_FIRST:
        zz = z_of(dz)
        got(na.at[xl * 8 + zz], n_zr.at[zz])
        send(na.at[xl * 8 + zz], na.at[xl * 8 + zz], n_xs.at[zz], n_xr.at[zz], x_dev)

    emb, values = time_embeds(steps)
    noise_levels = values / 1000.0
    l_gtw.wait()
    gg[...] = dot(emb, tw_gen[...])
    l_tt.wait()
    l_ct.wait()

    def modulate(i, carry):
        md[i // 3, lax.rem(i, 3)] = dot(emb, tw[i // 3, lax.rem(i, 3)])
        return carry

    lax.fori_loop(0, 6, modulate, 0)
    l_resid.wait()

    total = sum_end(p1f, x1r, a_xr, z1r, a_zr)
    latent = (resid[...].astype(F32) + gg[0:1, :] * total).astype(BF16)
    la[s] = latent
    lat4[r] = latent

    for dz in NEAR_FIRST:
        send(la.at[s], la.at[s], l_zs.at[dz], l_zr.at[z], z_dev(dz))
    send(la.at[s], la.at[s], l_xs.at[z], l_xr.at[z], x_dev)
    for d in (1, 2, 3):
        send(lat4.at[r], lat4.at[r], l_ys.at[d], l_yr.at[r], y_dev(d))
    for level in range(2):
        for model in range(2):
            first = lax.broadcasted_iota(jnp.int32, (16, 1280), 0) == 0
            shift = md[model, 0, 1 + level : 2 + level, :]
            sc[level, model, 256:272, :] = jnp.where(first, shift, 0.0).astype(BF16)

    def prepare(b):
        rows = pl.ds(pl.multiple_of(b * 16, 16), 16)
        lat = la[b].astype(F32)
        noi = na[b].astype(F32)
        for level in range(2):
            sl = noise_levels[1 + level : 2 + level, 0:1]
            noisy = ((1.0 - sl) * lat + sl * noi).astype(BF16).astype(F32)
            square = jnp.sum(noisy * noisy, axis=1, keepdims=True)
            sqc[level, rows, :] = jnp.broadcast_to(square, (16, 128))
            for model in range(2):
                scale = 1.0 + md[model, 1, 1 + level : 2 + level, :]
                sc[level, model, rows, :] = (noisy * scale).astype(BF16)

    prepare(s)
    for dz in NEAR_FIRST:
        zz = z_of(dz)
        b = xl * 8 + zz
        got(la.at[b], l_zr.at[zz])
        send(la.at[b], la.at[b], l_xs.at[zz], l_xr.at[zz], x_dev)
        prepare(b)
    for dz in (0,) + NEAR_FIRST:
        zz = z_of(dz)
        b = ol * 8 + zz
        got(la.at[b], l_xr.at[zz])
        got(na.at[b], n_xr.at[zz])
        prepare(b)

    l_tq.wait()
    l_cq.wait()

    def qkv_dots(k):
        kind = (k + 1) % 3
        for level in range(2):
            cs[k, level] = dot(sc[level, oc], wq[oc, kind]).astype(BF16)
            send(cs.at[k, level], cr.at[k, level], c_s.at[k, level], c_r.at[k, level], core_dev)
        for level in range(2):
            of[k % 2, level] = dot(sc[level, c], wq[c, kind])

    def qkv_sums(k):
        for level in range(2):
            got(cr.at[k, level], c_r.at[k, level])
            xs[k, level] = (of[k % 2, level] + cr[k, level].astype(F32)).astype(BF16)
            send(xs.at[k, level], xr.at[k, xh], x_s.at[k, level], x_r.at[k, xh], side_dev(level))

    for level in range(2):
        row = jnp.transpose(sqc[level])[0:8, :]
        sqs[level] = row
    send(sqs, cqr, q_s.at[0], q_r.at[0], core_dev)
    qkv_dots(0)
    got(cqr, q_r.at[0])
    sqx[...] = sqs[...] + cqr[...]
    for level in range(2):
        send(sqx.at[level], xqr.at[xh], q_s.at[1 + level], q_r.at[1 + xh], side_dev(level))
    qkv_dots(1)
    qkv_sums(0)
    qkv_dots(2)
    qkv_sums(1)
    qkv_sums(2)

    for i in range(2):
        got(xqr.at[i], q_r.at[1 + i])
    square = jnp.broadcast_to((xqr[0] + xqr[1])[0:1, :], (128, 256))
    rinv = lax.rsqrt(jnp.transpose(square) * (1.0 / D) + 1e-06)
    for i in range(2):
        got(nrm.at[i], m_r.at[i])

    def mixed_head(k, h):
        cols = slice(h * 128, h * 128 + 128)
        both = xr[k, 0, :, cols].astype(F32) + xr[k, 1, :, cols].astype(F32)
        return both[0:256] * rinv + both[256:257]

    def normed(values, gains):
        factor = lax.rsqrt(jnp.mean(values * values, axis=-1, keepdims=True) + 1e-06)
        return (values * factor * gains).astype(BF16)

    for k in range(2):
        for i in range(2):
            got(xr.at[k, i], x_r.at[k, i])
        for h in range(2):
            cols = slice(h * 128, h * 128 + 128)
            values = mixed_head(k, h)
            if k == 0:
                values = normed(values, nrm[c, 1:2, cols])
            kvb[k, r, :, cols] = values.astype(BF16)
        for d in (1, 3):
            send(kvb.at[k, r], kvb.at[k, r], kv_s.at[k, d], kv_r.at[k, r], y_dev(d))
    for i in range(2):
        got(xr.at[2, i], x_r.at[2, i])
    for h in range(2):
        cols = slice(h * 128, h * 128 + 128)
        qb[h] = normed(mixed_head(2, h), nrm[c, 0:1, cols])
    below, above, across = y_of(3), y_of(1), y_of(2)
    got(kvb.at[0, below], kv_r.at[0, below])
    send(kvb.at[0, below], kvb.at[0, below], kv_s.at[0, 2], kv_r.at[0, below], y_dev(1))
    got(kvb.at[0, above], kv_r.at[0, above])
    got(kvb.at[1, above], kv_r.at[1, above])
    send(kvb.at[1, above], kvb.at[1, above], kv_s.at[1, 2], kv_r.at[1, above], y_dev(3))

    exponent = math.log2(math.e) / math.sqrt(HEAD_DIM)
    sums = [jnp.zeros((256, 1), F32)] * 2
    outs = [jnp.zeros((256, 128), F32)] * 2
    for n, b in enumerate((r, above, below, across)):
        if n == 2:
            got(kvb.at[1, below], kv_r.at[1, below])
        if n == 3:
            got(kvb.at[0, across], kv_r.at[0, across])
            got(kvb.at[1, across], kv_r.at[1, across])
        for h in range(2):
            cols = slice(h * 128, h * 128 + 128)
            e = jnp.exp2(dot_t(qb[h], kvb[0, b, :, cols]) * exponent)
            sums[h] = sums[h] + jnp.sum(e, axis=1, keepdims=True)
            outs[h] = outs[h] + dot(e.astype(BF16), kvb[1, b, :, cols])
    for h in range(2):
        hos[:, h * 128 : h * 128 + 128] = (outs[h] / sums[h]).astype(BF16)
    for level in range(2):
        send(hos, ha.at[xh, c], h_s.at[level], h_r.at[xh, c], side_dev(level))

    l_to.wait()
    l_co.wait()

    def out_term(level, model, half):
        sign = (model.astype(F32) - 0.5) * md[model, 2, 1 + level : 2 + level, :]
        return sign * dot(ha[level, model, pl.ds(pl.multiple_of(half * 128, 128), 128)], ow[model])

    for level in range(2):
        got(ha.at[level, c], h_r.at[level, c])
        send(ha.at[level, c], ha.at[level, c], h_s.at[2 + level], h_r.at[level, c], core_dev)
    for half in range(2):
        acc[half] = out_term(0, c, half) + out_term(1, c, half)
    for level in range(2):
        got(ha.at[level, oc], h_r.at[level, oc])
    p2b[...] = (acc[ol] + out_term(0, oc, ol) + out_term(1, oc, ol)).astype(BF16).reshape(8, 16, 1280)
    sum_start(p2b, x2r, b_xs, b_xr)
    p1f[...] = (acc[xl] + out_term(0, oc, xl) + out_term(1, oc, xl)).reshape(8, 16, 1280)
    sum_middle(p1f, x2r, b_xr, z2s, z2r, b_zs, b_zr)
    for d in (1, 2, 3):
        got(lat4.at[y_of(d)], l_yr.at[y_of(d)])
    latent_out[...] = lat4[...].reshape(64, 1280)
    total = sum_end(p1f, x2r, b_xr, z2r, b_zr)
    grad[...] = (gg[0:1, :] * total).astype(BF16)

    for d in (2, 1, 3):
        src = grad.at[:, pl.ds(column_start(y_of(d)), 384)]
        send(src, ga.at[s, r], g_ys.at[d], g_yr.at[r], y_dev(d))
    ga[s, r] = grad[:, pl.ds(column_start(r), 384)]
    for d in (1, 3, 2):
        got(ga.at[s, y_of(d)], g_yr.at[y_of(d)])
    for dz in NEAR_FIRST:
        send(ga.at[s], ga.at[s], g_zs.at[dz], g_zr.at[z], z_dev(dz))
    send(ga.at[s], ga.at[s], g_xs.at[z], g_xr.at[z], x_dev)
    for dz in NEAR_FIRST:
        zz = z_of(dz)
        b = xl * 8 + zz
        got(ga.at[b], g_zr.at[zz])
        send(ga.at[b], ga.at[b], g_xs.at[zz], g_xr.at[zz], x_dev)
    l_all.wait()

    def grad_term(half):
        lhs = heads[pl.ds(half * 8, 8)].reshape(512, 256)
        rhs = ga[pl.ds(half * 8, 8)].reshape(512, 384)
        return lax.dot_general(lhs, rhs, (((0,), (0,)), ((), ())), preferred_element_type=F32)

    first_half = grad_term(xl)
    for dz in range(8):
        zz = z_of(dz)
        got(ga.at[ol * 8 + zz], g_xr.at[zz])
    wga[r] = (first_half + grad_term(ol)).astype(BF16).reshape(2, 128, 384)
    for i, d in ((0, 1), (1, 3), (1, 1), (0, 3)):
        send(wga.at[r, i], wga.at[r, i], w_s.at[i, d], w_r.at[i, r], y_dev(d))
    got(wga.at[below, 0], w_r.at[0, below])
    send(wga.at[below, 0], wga.at[below, 0], w_s.at[0, 2], w_r.at[0, below], y_dev(1))
    got(wga.at[above, 1], w_r.at[1, above])
    send(wga.at[above, 1], wga.at[above, 1], w_s.at[1, 2], w_r.at[1, above], y_dev(3))
    got(wga.at[below, 1], w_r.at[1, below])
    got(wga.at[above, 0], w_r.at[0, above])
    got(wga.at[across, 0], w_r.at[0, across])
    got(wga.at[across, 1], w_r.at[1, across])
    for i in range(2):
        rows = slice(i * 128, i * 128 + 128)
        grad_out[rows, 0:384] = wga[0, i]
        grad_out[rows, 384:768] = wga[1, i]
        grad_out[rows, 768:1024] = wga[2, i, :, 128:384]
        grad_out[rows, 1024:1280] = wga[3, i, :, 128:384]
    for copy in sent:
        copy.wait_send()


def on_device(
    gen_heads,
    gen_resid,
    gen_out_w,
    gen_time_w,
    noise,
    steps,
    teacher_qkv,
    teacher_out,
    teacher_time,
    teacher_norm,
    critic_qkv,
    critic_out,
    critic_time,
    critic_norm,
):
    vmem = pl.BlockSpec(memory_space=pltpu.VMEM)
    hbm = pl.BlockSpec(memory_space=pl.ANY)
    V = pltpu.VMEM
    S = pltpu.SemaphoreType.DMA
    block = (16, 1280)
    scratch = [
        V((16, 16, 256), BF16), V((16, 4, 16, 256), BF16), V((256, 1280), BF16),
        V((256, 1280), BF16), V(block, BF16), V((2, 3, 1280, 256), BF16),
        V((2, 256, 1280), BF16), V((2, 3, 256, 1280), BF16), V((2, 2, 256), F32),
        V((8, 1280), F32), V((2, 3, 8, 1280), F32),
        V((8,) + block, BF16), V((8,) + block, F32), V((8,) + block, BF16),
        V((8,) + block, BF16), V((8,) + block, BF16),
        V((16,) + block, BF16), V((16,) + block, BF16), V((4,) + block, BF16),
        V((2, 2, 272, 1280), BF16), V((2, 256, 128), F32),
        V((2, 8, 256), F32), V((2, 8, 256), F32), V((2, 8, 256), F32), V((2, 8, 256), F32),
        V((3, 2, 272, 256), BF16), V((3, 2, 272, 256), BF16), V((2, 2, 272, 256), F32),
        V((3, 2, 272, 256), BF16), V((3, 2, 272, 256), BF16),
        V((2, 4, 256, 256), BF16), V((2, 256, 128), BF16), V((256, 256), BF16),
        V((2, 2, 256, 256), BF16),
        V((2, 128, 1280), F32), V((8,) + block, BF16), V((8,) + block, BF16),
        V((8,) + block, BF16), V((8,) + block, BF16),
        V(block, BF16), V((16, 4, 16, 384), BF16), V((4, 2, 128, 384), BF16),
        S((12,)),
        S((8,)), S((8,)), S((8,)), S((8,)),
        S((8,)), S((8,)), S((8,)), S((8,)),
        S((8,)), S((8,)), S((8,)), S((8,)), S((4,)), S((4,)),
        S((8,)), S((8,)), S((8,)), S((8,)),
        S((4,)), S((4,)), S((8,)), S((8,)), S((8,)), S((8,)),
        S((2,)), S((2,)), S((3,)), S((3,)), S((3, 2)), S((3, 2)), S((3, 2)), S((3, 2)),
        S((2, 4)), S((2, 4)), S((4,)), S((2, 2)), S((2, 4)), S((2, 4)),
    ]
    latent, weight_grad = pl.pallas_call(
        kernel,
        out_shape=(
            jax.ShapeDtypeStruct((64, 1280), BF16),
            jax.ShapeDtypeStruct((256, 1280), BF16),
        ),
        in_specs=[hbm] * 5 + [pl.BlockSpec(memory_space=pltpu.SMEM)] + [hbm] * 6 + [vmem] * 2,
        out_specs=(vmem, vmem),
        scratch_shapes=scratch,
        compiler_params=pltpu.CompilerParams(
            collective_id=0, has_side_effects=True, vmem_limit_bytes=60 * 1024 * 1024
        ),
        name="step",
    )(
        gen_heads.reshape(16, 4, 16, 256),
        gen_resid.reshape(4, 16, 1280),
        gen_out_w,
        gen_time_w,
        noise.reshape(4, 16, 1280),
        steps,
        teacher_qkv.transpose(1, 0, 2),
        critic_qkv.transpose(1, 0, 2),
        teacher_out,
        critic_out,
        teacher_time.transpose(1, 0, 2),
        critic_time.transpose(1, 0, 2),
        teacher_norm,
        critic_norm,
    )
    return (latent, weight_grad)


def solution(mesh):
    in_specs = (
        P(None, "seq"),
        P("seq", "mp"),
        P("seq", "mp"),
        P(None, "mp"),
        P("seq", "mp"),
        P(),
        P("mp", None, "seq"),
        P("seq", "mp"),
        P(None, None, "mp"),
        P(None, "seq"),
        P("mp", None, "seq"),
        P("seq", "mp"),
        P(None, None, "mp"),
        P(None, "seq"),
    )
    out_specs = (P("seq", "mp"), P("seq", "mp"))
    return jax.shard_map(
        on_device, mesh=mesh, in_specs=in_specs, out_specs=out_specs, check_vma=False
    )
```

```python
import math

import jax
import jax.numpy as jnp
from jax import lax
from jax.experimental import pallas as pl
from jax.experimental.pallas import tpu as pltpu
from jax.sharding import PartitionSpec as P

D = 5120
HEAD_DIM = 128
BF16 = jnp.bfloat16
F32 = jnp.float32
MESH = pl.DeviceIdType.MESH
FAR_FIRST = (4, 3, 5, 2, 6, 1, 7)
NEAR_FIRST = (1, 7, 2, 6, 3, 5, 4)


def time_embeds(steps):
    row = lax.broadcasted_iota(jnp.int32, (8, 128), 0)
    values = jnp.where(row == 0, steps[0], jnp.where(row == 1, steps[1], steps[2])).astype(F32)
    positions = lax.broadcasted_iota(jnp.int32, (8, 128), 1).astype(F32)
    angles = values * jnp.exp(positions * (-math.log(10000.0) / 128))
    return jnp.concatenate([jnp.cos(angles), jnp.sin(angles)], axis=1).astype(BF16), values


def dot(a, b):
    return jnp.dot(a, b, preferred_element_type=F32)


def dot_t(a, b):
    return lax.dot_general(a, b, (((1,), (1,)), ((), ())), preferred_element_type=F32)


FRONT = ((0, 768), (768, 512))
NOISE_AT = 0
KVD = False
QO = 1
DIRECT15 = False
TAIL = ((0, 3, 6, 8), (1, 4, 7, 9), (2, 5))


def cols(i, n=1):
    return slice(i * 128, (i + n) * 128)


def kernel(
    gh4, resid4, gow, gtw, noise4, steps, tq, cq, tow, cow, ttw, ctw, t_norm, c_norm,
    latent_out, grad_out,
    heads_r, heads, ow_gen, tw_gen, resid, wq, ow, tw, nrm, gg, md,
    na, lat4, sc, sqc, sqs, cqr, sqx, xqr,
    cs, cr, of, pre, xs, xr, kvb, qb, hos, ha, acc,
    front, tail,
    lsem, n_zs, n_zr, n_xs, n_xr, l_ys, l_yr,
    m_s, m_r, q_s, q_r, c_s, c_r, x_s, x_r, kv_s, kv_r, h_s, h_r,
):
    r = lax.axis_index("role")
    s = lax.axis_index("seq")
    m = lax.axis_index("mp")
    xl, z = s // 8, lax.rem(s, 8)
    xh, c = m // 2, lax.rem(m, 2)
    ol = 1 - xl
    oc = 1 - c
    z_of = lambda dz: lax.rem(z + dz, 8)
    z_dev = lambda dz: {"seq": xl * 8 + z_of(dz)}
    x_dev = {"seq": ol * 8 + z}
    core_dev = {"mp": 2 * xh + oc}
    side_dev = lambda level: {"seq": ol * 8 + z, "mp": 2 * level + c}
    y_of = lambda d: lax.rem(r + d, 4)
    y_dev = lambda d: {"role": y_of(d)}
    below, above, across = y_of(3), y_of(1), y_of(2)
    pair, odd = r // 2, lax.rem(r, 2)
    pair_dev = {"role": 2 * pair + 1 - odd}

    def rc(src, dst, ssem, rsem, dev):
        return pltpu.make_async_remote_copy(
            src_ref=src, dst_ref=dst, send_sem=ssem, recv_sem=rsem,
            device_id=dev, device_id_type=MESH,
        )

    sent = []

    def send(*args):
        copy = rc(*args)
        copy.start()
        sent.append(copy)

    def got(dst, rsem):
        rc(dst, dst, rsem, rsem, x_dev).wait_recv()

    loads = []

    def load(src, dst):
        copy = pltpu.make_async_copy(src, dst, lsem.at[len(loads)])
        copy.start()
        loads.append(copy)
        return copy

    barrier = pltpu.get_barrier_semaphore()
    peers = [z_dev(dz) for dz in range(1, 8)] + [x_dev, core_dev]
    peers += [side_dev(1 - xh)] + [y_dev(d) for d in (1, 2, 3)]
    for dev in peers:
        pl.semaphore_signal(barrier, inc=1, device_id=dev, device_id_type=MESH)
    l_heads = load(gh4.at[:, r], heads_r)
    l_gow = load(gow, ow_gen)
    l_noise = load(noise4.at[r], na.at[s])
    l_resid = load(resid4.at[r], resid)
    l_gtw = load(gtw, tw_gen)
    l_tt = load(ttw, tw.at[0])
    l_ct = load(ctw, tw.at[1])
    l_tq = load(tq, wq.at[0])
    l_cq = load(cq, wq.at[1])
    l_to = load(tow, ow.at[0])
    l_co = load(cow, ow.at[1])
    l_all = load(gh4, heads)
    l_heads.wait()
    l_gow.wait()
    l_noise.wait()
    part = dot(heads_r[pl.ds(ol * 8, 8)].reshape(128, 256), ow_gen[...])
    for f, (start, width) in zip(front, FRONT):
        f["pb"][...] = part[:, start : start + width].astype(BF16).reshape(8, 16, width)
    pl.semaphore_wait(barrier, len(peers))

    def sum_start(f):
        for dz in FAR_FIRST + (0,):
            zz = z_of(dz)
            send(f["pb"].at[zz], f["xr"].at[zz], f["xs_s"].at[zz], f["xs_r"].at[zz], x_dev)

    def sum_middle(f):
        for dz in FAR_FIRST:
            zz = z_of(dz)
            got(f["xr"].at[zz], f["xs_r"].at[zz])
            f["zs"][zz] = (f["pf"][zz] + f["xr"][zz].astype(F32)).astype(BF16)
            send(f["zs"].at[zz], f["zr"].at[z], f["zs_s"].at[dz], f["zs_r"].at[z], z_dev(dz))

    def sum_end(f):
        got(f["xr"].at[z], f["xs_r"].at[z])
        total = f["pf"][z] + f["xr"][z].astype(F32)
        for dz in NEAR_FIRST:
            zz = z_of(dz)
            got(f["zr"].at[zz], f["zs_r"].at[zz])
            total = total + f["zr"][zz].astype(F32)
        return total

    def gather_start(f):
        own = f["ga"].at[s]
        for dz in NEAR_FIRST:
            send(own, own, f["gz_s"].at[dz], f["gz_r"].at[z], z_dev(dz))
        send(own, own, f["gx_s"].at[z], f["gx_r"].at[z], x_dev)

    def gather_step(f, dz):
        zz = z_of(dz)
        block = f["ga"].at[xl * 8 + zz]
        got(block, f["gz_r"].at[zz])
        send(block, block, f["gx_s"].at[zz], f["gx_r"].at[zz], x_dev)
        return xl * 8 + zz

    def gather_end(f, dz):
        zz = z_of(dz)
        got(f["ga"].at[ol * 8 + zz], f["gx_r"].at[zz])
        return ol * 8 + zz

    def noise_start():
        for dz in NEAR_FIRST:
            send(na.at[s], na.at[s], n_zs.at[dz], n_zr.at[z], z_dev(dz))

    if NOISE_AT == 0:
        noise_start()
    for f in front:
        sum_start(f)
    for i, norm in enumerate((t_norm, c_norm)):
        send(norm, nrm.at[i], m_s.at[i], m_r.at[i], x_dev)
    if NOISE_AT == 1:
        noise_start()
    send(na.at[s], na.at[s], n_xs.at[z], n_xr.at[z], x_dev)
    part = dot(heads_r[pl.ds(xl * 8, 8)].reshape(128, 256), ow_gen[...])
    for f, (start, width) in zip(front, FRONT):
        f["pf"][...] = part[:, start : start + width].reshape(8, 16, width)
    for n, f in enumerate(front):
        sum_middle(f)
        if n == 0 and NOISE_AT == 2:
            noise_start()
    if NOISE_AT == 3:
        noise_start()

    emb, values = time_embeds(steps)
    noise_levels = values / 1000.0
    l_gtw.wait()
    gg[...] = dot(emb, tw_gen[...])
    l_tt.wait()
    l_ct.wait()

    def modulate(i, carry):
        md[i // 3, lax.rem(i, 3)] = dot(emb, tw[i // 3, lax.rem(i, 3)])
        return carry

    lax.fori_loop(0, 6, modulate, 0)
    l_resid.wait()

    def noise_forward():
        for dz in NEAR_FIRST:
            zz = z_of(dz)
            got(na.at[xl * 8 + zz], n_zr.at[zz])
            send(na.at[xl * 8 + zz], na.at[xl * 8 + zz], n_xs.at[zz], n_xr.at[zz], x_dev)

    if NOISE_AT < 2:
        noise_forward()

    for f, (start, width) in zip(front, FRONT):
        at = slice(start, start + width)
        latent = (resid[:, at].astype(F32) + gg[0:1, at] * sum_end(f)).astype(BF16)
        f["ga"][s] = latent
        lat4[r, :, at] = latent
        gather_start(f)
    if NOISE_AT >= 2:
        noise_forward()
    for d in (1, 2, 3):
        send(lat4.at[r], lat4.at[r], l_ys.at[d], l_yr.at[r], y_dev(d))
    for level in range(2):
        for model in range(2):
            first = lax.broadcasted_iota(jnp.int32, (16, 1280), 0) == 0
            shift = md[model, 0, 1 + level : 2 + level, :]
            sc[level, model, 256:272, :] = jnp.where(first, shift, 0.0).astype(BF16)

    def prepare(f, start, width, b):
        at = slice(start, start + width)
        rows = pl.ds(pl.multiple_of(b * 16, 16), 16)
        lat = f["ga"][b].astype(F32)
        noi = na[b, :, at].astype(F32)
        for level in range(2):
            sl = noise_levels[1 + level : 2 + level, 0:1]
            noisy = ((1.0 - sl) * lat + sl * noi).astype(BF16).astype(F32)
            square = jnp.sum(noisy * noisy, axis=1, keepdims=True)
            square = jnp.broadcast_to(square, (16, 128))
            if start == 0:
                sqc[level, rows, :] = square
            else:
                sqc[level, rows, :] += square
            for model in range(2):
                scale = 1.0 + md[model, 1, 1 + level : 2 + level, at]
                sc[level, model, rows, at] = (noisy * scale).astype(BF16)

    for f, (start, width) in zip(front, FRONT):
        prepare(f, start, width, s)
        for dz in NEAR_FIRST:
            prepare(f, start, width, gather_step(f, dz))
    for dz in range(8):
        got(na.at[ol * 8 + z_of(dz)], n_xr.at[z_of(dz)])
    l_tq.wait()
    l_cq.wait()

    def product_part(level, model, kind, n):
        at = slice(FRONT[n][0], sum(FRONT[n]))
        return dot(sc[level, model, :, at], wq[model, kind, at])

    for n, (f, (start, width)) in enumerate(zip(front, FRONT)):
        for dz in (0,) + NEAR_FIRST:
            prepare(f, start, width, gather_end(f, dz))
        if n == 0:
            for level in range(2):
                pre[level] = product_part(level, oc, 1, 0)
                of[0, level] = product_part(level, c, 1, 0)

    def qkv_dots(k):
        kind = (k + 1) % 3
        for level in range(2):
            if k == 0:
                cs[k, level] = (pre[level] + product_part(level, oc, 1, 1)).astype(BF16)
            else:
                cs[k, level] = dot(sc[level, oc], wq[oc, kind]).astype(BF16)
            send(cs.at[k, level], cr.at[k, level], c_s.at[k, level], c_r.at[k, level], core_dev)
        for level in range(2):
            if k == 0:
                of[k, level] += product_part(level, c, 1, 1)
            else:
                of[k % 2, level] = dot(sc[level, c], wq[c, kind])

    def qkv_sums(k):
        for level in range(2):
            got(cr.at[k, level], c_r.at[k, level])
            xs[k, level] = (of[k % 2, level] + cr[k, level].astype(F32)).astype(BF16)
            send(xs.at[k, level], xr.at[k, xh], x_s.at[k, level], x_r.at[k, xh], side_dev(level))

    def square_send():
        for level in range(2):
            sqs[level] = jnp.transpose(sqc[level])[0:8, :]
        send(sqs, cqr, q_s.at[0], q_r.at[0], core_dev)

    def square_pass():
        got(cqr, q_r.at[0])
        sqx[...] = sqs[...] + cqr[...]
        for level in range(2):
            send(sqx.at[level], xqr.at[xh], q_s.at[1 + level], q_r.at[1 + xh], side_dev(level))

    if QO == 0:
        square_send()
        qkv_dots(0)
        square_pass()
        qkv_dots(1)
        qkv_sums(0)
        qkv_dots(2)
        qkv_sums(1)
        qkv_sums(2)
    else:
        qkv_dots(0)
        square_send()
        qkv_sums(0)
        qkv_dots(1)
        square_pass()
        qkv_sums(1)
        qkv_dots(2)
        qkv_sums(2)

    for i in range(2):
        got(xqr.at[i], q_r.at[1 + i])
    square = jnp.broadcast_to((xqr[0] + xqr[1])[0:1, :], (128, 256))
    rinv = lax.rsqrt(jnp.transpose(square) * (1.0 / D) + 1e-06)
    for i in range(2):
        got(nrm.at[i], m_r.at[i])

    def mixed_head(k, h):
        both = xr[k, 0, :, cols(h)].astype(F32) + xr[k, 1, :, cols(h)].astype(F32)
        return both[0:256] * rinv + both[256:257]

    def normed(values, gains):
        factor = lax.rsqrt(jnp.mean(values * values, axis=-1, keepdims=True) + 1e-06)
        return (values * factor * gains).astype(BF16)

    for k in range(2):
        for i in range(2):
            got(xr.at[k, i], x_r.at[k, i])
        for h in range(2):
            values = mixed_head(k, h)
            if k == 0:
                values = normed(values, nrm[c, 1:2, cols(h)])
            kvb[k, r, :, cols(h)] = values.astype(BF16)
        for d in (1, 3, 2) if KVD else (1, 3):
            send(kvb.at[k, r], kvb.at[k, r], kv_s.at[k, d], kv_r.at[k, r], y_dev(d))
    got(kvb.at[0, below], kv_r.at[0, below])
    if not KVD:
        send(kvb.at[0, below], kvb.at[0, below], kv_s.at[0, 2], kv_r.at[0, below], y_dev(1))
    for i in range(2):
        got(xr.at[2, i], x_r.at[2, i])
    for h in range(2):
        qb[h] = normed(mixed_head(2, h), nrm[c, 0:1, cols(h)])
    got(kvb.at[1, above], kv_r.at[1, above])
    if not KVD:
        send(kvb.at[1, above], kvb.at[1, above], kv_s.at[1, 2], kv_r.at[1, above], y_dev(3))
    got(kvb.at[0, above], kv_r.at[0, above])

    exponent = math.log2(math.e) / math.sqrt(HEAD_DIM)
    sums = [jnp.zeros((256, 1), F32)] * 2
    outs = [jnp.zeros((256, 128), F32)] * 2
    for n, b in enumerate((r, above, below, across)):
        if n == 2:
            got(kvb.at[1, below], kv_r.at[1, below])
        if n == 3:
            got(kvb.at[0, across], kv_r.at[0, across])
            got(kvb.at[1, across], kv_r.at[1, across])
        for h in range(2):
            e = jnp.exp2(dot_t(qb[h], kvb[0, b, :, cols(h)]) * exponent)
            sums[h] = sums[h] + jnp.sum(e, axis=1, keepdims=True)
            outs[h] = outs[h] + dot(e.astype(BF16), kvb[1, b, :, cols(h)])
            if n == 3:
                hos[h] = (outs[h] / sums[h]).astype(BF16)
                for level in range(2):
                    send(hos.at[h], ha.at[xh, c, h], h_s.at[level, h], h_r.at[xh, c, h], side_dev(level))

    l_to.wait()
    l_co.wait()

    def out_term(level, model, half):
        rows = pl.ds(pl.multiple_of(half * 128, 128), 128)
        both = jnp.concatenate([ha[level, model, h, rows] for h in range(2)], axis=1)
        sign = (model.astype(F32) - 0.5) * md[model, 2, 1 + level : 2 + level, :]
        return sign * dot(both, ow[model])

    for h in range(2):
        for level in range(2):
            block = ha.at[level, c, h]
            got(block, h_r.at[level, c, h])
            send(block, block, h_s.at[2 + level, h], h_r.at[level, c, h], core_dev)
    for half in range(2):
        acc[half] = out_term(0, c, half) + out_term(1, c, half)
    for h in range(2):
        for level in range(2):
            got(ha.at[level, oc, h], h_r.at[level, oc, h])

    def by_chunk(part, name):
        for f, tiles in zip(tail, TAIL):
            for i, tile in enumerate(tiles):
                piece = part[:, cols(tile)].reshape(8, 16, 128)
                f[name][:, :, cols(i)] = piece.astype(f[name].dtype)

    by_chunk(acc[ol] + out_term(0, oc, ol) + out_term(1, oc, ol), "pb")
    for f in tail:
        sum_start(f)
    by_chunk(acc[xl] + out_term(0, oc, xl) + out_term(1, oc, xl), "pf")
    for f in tail:
        sum_middle(f)
    for d in (1, 2, 3):
        got(lat4.at[y_of(d)], l_yr.at[y_of(d)])
    latent_out[...] = lat4[...].reshape(64, 1280)

    def finish(n):
        f, tiles = tail[n], TAIL[n]
        total = sum_end(f)
        for i, tile in enumerate(tiles):
            f["grad"][i] = (gg[0:1, cols(tile)] * total[:, cols(i)]).astype(BF16)
        if n < 2:
            for d in (2, 1, 3):
                send(f["grad"].at[y_of(d)], f["ga"].at[s, r], f["y_s"].at[d], f["y_r"].at[r], y_dev(d))
            f["ga"][s, r] = f["grad"][r]
        else:
            send(f["grad"].at[1 - odd], f["ga"].at[s, odd], f["y_s"].at[0], f["y_r"].at[odd], pair_dev)
            f["ga"][s, odd] = f["grad"][odd]

    def collect(n):
        f = tail[n]
        if n < 2:
            for d in (1, 3, 2):
                got(f["ga"].at[s, y_of(d)], f["y_r"].at[y_of(d)])
        else:
            got(f["ga"].at[s, 1 - odd], f["y_r"].at[1 - odd])
        gather_start(f)

    def grad_term(n, half):
        at = pl.ds(half * 8, 8)
        lhs = heads[at] if n < 2 else heads[at, pl.ds(2 * pair, 2)]
        rows = 512 if n < 2 else 256
        return lax.dot_general(
            lhs.reshape(rows, 256), tail[n]["ga"][at].reshape(rows, 128),
            (((0,), (0,)), ((), ())), preferred_element_type=F32,
        )

    def product(n):
        f = tail[n]
        half = grad_term(n, xl)
        for dz in range(8):
            gather_end(f, dz)
        f["wg"][r] = (half + grad_term(n, ol)).astype(BF16)
        for d in (2, 1, 3):
            send(f["wg"].at[r], f["wg"].at[r], f["w_s"].at[d], f["w_r"].at[r], y_dev(d))

    def arrived(n):
        f = tail[n]
        for b in (below, above, across):
            got(f["wg"].at[b], f["w_r"].at[b])

    finish(0)
    collect(0)
    finish(1)
    for dz in NEAR_FIRST[:3]:
        gather_step(tail[0], dz)
    collect(1)
    finish(2)
    for dz in NEAR_FIRST[3:]:
        gather_step(tail[0], dz)
    collect(2)
    l_all.wait()
    for dz in NEAR_FIRST:
        gather_step(tail[1], dz)
    product(0)
    for dz in NEAR_FIRST:
        gather_step(tail[2], dz)
    product(1)
    product(2)
    arrived(0)
    arrived(1)
    for n in range(2):
        for i, tile in enumerate(TAIL[n]):
            grad_out[:, cols(tile)] = tail[n]["wg"][i]
    arrived(2)
    for i, tile in enumerate(TAIL[2]):
        both = tail[2]["wg"][i].astype(F32) + tail[2]["wg"][i + 2].astype(F32)
        grad_out[:, cols(tile)] = both.astype(BF16)
    for copy in sent:
        copy.wait_send()


def hand_over(latent, weight_grad, latent_out, grad_out):
    latent_out[...] = latent[...]
    grad_out[...] = weight_grad[...]


def on_device(
    gen_heads,
    gen_resid,
    gen_out_w,
    gen_time_w,
    noise,
    steps,
    teacher_qkv,
    teacher_out,
    teacher_time,
    teacher_norm,
    critic_qkv,
    critic_out,
    critic_time,
    critic_norm,
):
    vmem = pl.BlockSpec(memory_space=pltpu.VMEM)
    hbm = pl.BlockSpec(memory_space=pl.ANY)
    V = pltpu.VMEM
    S = pltpu.SemaphoreType.DMA
    block = (16, 1280)
    sums = lambda width: {
        "pb": V((8, 16, width), BF16), "pf": V((8, 16, width), F32),
        "xr": V((8, 16, width), BF16), "zs": V((8, 16, width), BF16), "zr": V((8, 16, width), BF16),
        "xs_s": S((8,)), "xs_r": S((8,)), "zs_s": S((8,)), "zs_r": S((8,)),
        "gz_s": S((8,)), "gz_r": S((8,)), "gx_s": S((8,)), "gx_r": S((8,)),
    }
    front = [{**sums(width), "ga": V((16, 16, width), BF16)} for _, width in FRONT]
    tail = [
        {
            **sums(128 * len(tiles)),
            "grad": V((len(tiles), 16, 128), BF16),
            "ga": V((16, len(tiles), 16, 128), BF16),
            "wg": V((4, 256, 128), BF16),
            "y_s": S((4,)), "y_r": S((4,)), "w_s": S((4,)), "w_r": S((4,)),
        }
        for tiles in TAIL
    ]
    scratch = [
        V((16, 16, 256), BF16), V((16, 4, 16, 256), BF16), V((256, 1280), BF16),
        V((256, 1280), BF16), V(block, BF16), V((2, 3, 1280, 256), BF16),
        V((2, 256, 1280), BF16), V((2, 3, 256, 1280), BF16), V((2, 2, 256), F32),
        V((8, 1280), F32), V((2, 3, 8, 1280), F32),
        V((16,) + block, BF16), V((4,) + block, BF16),
        V((2, 2, 272, 1280), BF16), V((2, 256, 128), F32),
        V((2, 8, 256), F32), V((2, 8, 256), F32), V((2, 8, 256), F32), V((2, 8, 256), F32),
        V((3, 2, 272, 256), BF16), V((3, 2, 272, 256), BF16), V((2, 2, 272, 256), F32), V((2, 272, 256), F32),
        V((3, 2, 272, 256), BF16), V((3, 2, 272, 256), BF16),
        V((2, 4, 256, 256), BF16), V((2, 256, 128), BF16), V((2, 256, 128), BF16),
        V((2, 2, 2, 256, 128), BF16), V((2, 128, 1280), F32),
        front, tail,
        S((12,)), S((8,)), S((8,)), S((8,)), S((8,)), S((4,)), S((4,)),
        S((2,)), S((2,)), S((3,)), S((3,)), S((3, 2)), S((3, 2)), S((3, 2)), S((3, 2)),
        S((2, 4)), S((2, 4)), S((4, 2)), S((2, 2, 2)),
    ]
    latent, weight_grad = pl.pallas_call(
        kernel,
        out_shape=(
            jax.ShapeDtypeStruct((64, 1280), BF16),
            jax.ShapeDtypeStruct((256, 1280), BF16),
        ),
        in_specs=[hbm] * 5 + [pl.BlockSpec(memory_space=pltpu.SMEM)] + [hbm] * 6 + [vmem] * 2,
        out_specs=(vmem, vmem),
        scratch_shapes=scratch,
        compiler_params=pltpu.CompilerParams(
            collective_id=0, has_side_effects=True, vmem_limit_bytes=60 * 1024 * 1024
        ),
        name="step",
    )(
        gen_heads.reshape(16, 4, 16, 256),
        gen_resid.reshape(4, 16, 1280),
        gen_out_w,
        gen_time_w,
        noise.reshape(4, 16, 1280),
        steps,
        teacher_qkv.transpose(1, 0, 2),
        critic_qkv.transpose(1, 0, 2),
        teacher_out,
        critic_out,
        teacher_time.transpose(1, 0, 2),
        critic_time.transpose(1, 0, 2),
        teacher_norm,
        critic_norm,
    )
    return pl.pallas_call(
        hand_over,
        out_shape=(
            jax.ShapeDtypeStruct((64, 1280), BF16),
            jax.ShapeDtypeStruct((256, 1280), BF16),
        ),
        in_specs=[vmem, vmem],
        out_specs=(vmem, vmem),
        compiler_params=pltpu.CompilerParams(vmem_limit_bytes=8 * 1024 * 1024),
        name="hand_over",
    )(latent, weight_grad)


def solution(mesh):
    in_specs = (
        P(None, "seq"),
        P("seq", "mp"),
        P("seq", "mp"),
        P(None, "mp"),
        P("seq", "mp"),
        P(),
        P("mp", None, "seq"),
        P("seq", "mp"),
        P(None, None, "mp"),
        P(None, "seq"),
        P("mp", None, "seq"),
        P("seq", "mp"),
        P(None, None, "mp"),
        P(None, "seq"),
    )
    out_specs = (P("seq", "mp"), P("seq", "mp"))
    return jax.shard_map(
        on_device, mesh=mesh, in_specs=in_specs, out_specs=out_specs, check_vma=False
    )
```

```python
import math

import jax
import jax.numpy as jnp
from jax import lax
from jax.experimental import pallas as pl
from jax.experimental.pallas import tpu as pltpu
from jax.sharding import PartitionSpec as P

D = 5120
HEAD_DIM = 128
BF16 = jnp.bfloat16
F32 = jnp.float32
MESH = pl.DeviceIdType.MESH
FAR_FIRST = (4, 3, 5, 2, 6, 1, 7)
NEAR_FIRST = (1, 7, 2, 6, 3, 5, 4)


def time_embeds(steps):
    row = lax.broadcasted_iota(jnp.int32, (8, 128), 0)
    values = jnp.where(row == 0, steps[0], jnp.where(row == 1, steps[1], steps[2])).astype(F32)
    positions = lax.broadcasted_iota(jnp.int32, (8, 128), 1).astype(F32)
    angles = values * jnp.exp(positions * (-math.log(10000.0) / 128))
    return jnp.concatenate([jnp.cos(angles), jnp.sin(angles)], axis=1).astype(BF16), values


def dot(a, b):
    return jnp.dot(a, b, preferred_element_type=F32)


def dot_t(a, b):
    return lax.dot_general(a, b, (((1,), (1,)), ((), ())), preferred_element_type=F32)


FRONT = ((0, 768), (768, 512))
NEAR, FAR = NEAR_FIRST[:4], NEAR_FIRST[4:]
TAIL = ((0, 3, 6, 8), (1, 4, 7, 9), (2, 5))


def cols(i, n=1):
    return slice(i * 128, (i + n) * 128)


def kernel(
    gh4, resid4, gow, gtw, noise4, steps, tq, cq, tow, cow, ttw, ctw, t_norm, c_norm,
    latent_out, grad_out,
    heads_r, heads, ow_gen, tw_gen, resid, wq, ow, tw, nrm, gg, md,
    na, lat4, sc, sqc, sqs, cqr, sqx, xqr,
    cs, cr, of, pre, xs, xr, kvb, qb, hos, ha, acc,
    front, tail,
    lsem, n_zs, n_zr, n_xs, n_xr, l_ys, l_yr,
    m_s, m_r, q_s, q_r, c_s, c_r, x_s, x_r, kv_s, kv_r, h_s, h_r,
):
    r = lax.axis_index("role")
    s = lax.axis_index("seq")
    m = lax.axis_index("mp")
    xl, z = s // 8, lax.rem(s, 8)
    xh, c = m // 2, lax.rem(m, 2)
    ol = 1 - xl
    oc = 1 - c
    z_of = lambda dz: lax.rem(z + dz, 8)
    z_dev = lambda dz: {"seq": xl * 8 + z_of(dz)}
    x_dev = {"seq": ol * 8 + z}
    core_dev = {"mp": 2 * xh + oc}
    side_dev = lambda level: {"seq": ol * 8 + z, "mp": 2 * level + c}
    y_of = lambda d: lax.rem(r + d, 4)
    y_dev = lambda d: {"role": y_of(d)}
    below, above, across = y_of(3), y_of(1), y_of(2)
    pair, odd = r // 2, lax.rem(r, 2)
    pair_dev = {"role": 2 * pair + 1 - odd}

    def rc(src, dst, ssem, rsem, dev):
        return pltpu.make_async_remote_copy(
            src_ref=src, dst_ref=dst, send_sem=ssem, recv_sem=rsem,
            device_id=dev, device_id_type=MESH,
        )

    sent = []

    def send(*args):
        copy = rc(*args)
        copy.start()
        sent.append(copy)

    def got(dst, rsem):
        rc(dst, dst, rsem, rsem, x_dev).wait_recv()

    loads = []

    def load(src, dst):
        copy = pltpu.make_async_copy(src, dst, lsem.at[len(loads)])
        copy.start()
        loads.append(copy)
        return copy

    barrier = pltpu.get_barrier_semaphore()
    peers = [z_dev(dz) for dz in range(1, 8)] + [x_dev, core_dev]
    peers += [side_dev(1 - xh)] + [y_dev(d) for d in (1, 2, 3)]
    for dev in peers:
        pl.semaphore_signal(barrier, inc=1, device_id=dev, device_id_type=MESH)
    l_heads = load(gh4.at[:, r], heads_r)
    l_gow = load(gow, ow_gen)
    l_noise = load(noise4.at[r], na.at[s])
    l_resid = load(resid4.at[r], resid)
    l_gtw = load(gtw, tw_gen)
    l_tt = load(ttw, tw.at[0])
    l_ct = load(ctw, tw.at[1])
    l_tq = load(tq, wq.at[0])
    l_cq = load(cq, wq.at[1])
    l_to = load(tow, ow.at[0])
    l_co = load(cow, ow.at[1])
    l_all = load(gh4, heads)
    l_heads.wait()
    l_gow.wait()
    l_noise.wait()
    part = dot(heads_r[pl.ds(ol * 8, 8)].reshape(128, 256), ow_gen[...])
    for f, (start, width) in zip(front, FRONT):
        f["pb"][...] = part[:, start : start + width].astype(BF16).reshape(8, 16, width)
    pl.semaphore_wait(barrier, len(peers))

    def sum_start(f):
        for dz in FAR_FIRST + (0,):
            zz = z_of(dz)
            send(f["pb"].at[zz], f["xr"].at[zz], f["xs_s"].at[zz], f["xs_r"].at[zz], x_dev)

    def sum_middle(f):
        for dz in FAR_FIRST:
            zz = z_of(dz)
            got(f["xr"].at[zz], f["xs_r"].at[zz])
            f["zs"][zz] = (f["pf"][zz] + f["xr"][zz].astype(F32)).astype(BF16)
            send(f["zs"].at[zz], f["zr"].at[z], f["zs_s"].at[dz], f["zs_r"].at[z], z_dev(dz))

    def sum_end(f):
        got(f["xr"].at[z], f["xs_r"].at[z])
        total = f["pf"][z] + f["xr"][z].astype(F32)
        for dz in NEAR_FIRST:
            zz = z_of(dz)
            got(f["zr"].at[zz], f["zs_r"].at[zz])
            total = total + f["zr"][zz].astype(F32)
        return total

    def gather_start(f):
        own = f["ga"].at[s]
        for dz in NEAR_FIRST:
            send(own, own, f["gz_s"].at[dz], f["gz_r"].at[z], z_dev(dz))
        send(own, own, f["gx_s"].at[z], f["gx_r"].at[z], x_dev)

    def gather_step(f, dz):
        zz = z_of(dz)
        block = f["ga"].at[xl * 8 + zz]
        got(block, f["gz_r"].at[zz])
        send(block, block, f["gx_s"].at[zz], f["gx_r"].at[zz], x_dev)
        return xl * 8 + zz

    def gather_end(f, dz):
        zz = z_of(dz)
        got(f["ga"].at[ol * 8 + zz], f["gx_r"].at[zz])
        return ol * 8 + zz

    def noise_start(distances):
        for dz in distances:
            send(na.at[s], na.at[s], n_zs.at[dz], n_zr.at[z], z_dev(dz))

    def noise_forward(distances):
        for dz in distances:
            zz = z_of(dz)
            got(na.at[xl * 8 + zz], n_zr.at[zz])
            send(na.at[xl * 8 + zz], na.at[xl * 8 + zz], n_xs.at[zz], n_xr.at[zz], x_dev)

    noise_start(NEAR)
    for f in front:
        sum_start(f)
    for i, norm in enumerate((t_norm, c_norm)):
        send(norm, nrm.at[i], m_s.at[i], m_r.at[i], x_dev)
    send(na.at[s], na.at[s], n_xs.at[z], n_xr.at[z], x_dev)
    part = dot(heads_r[pl.ds(xl * 8, 8)].reshape(128, 256), ow_gen[...])
    for f, (start, width) in zip(front, FRONT):
        f["pf"][...] = part[:, start : start + width].reshape(8, 16, width)
    for f in front:
        sum_middle(f)
    noise_start(FAR)
    noise_forward(NEAR)

    emb, values = time_embeds(steps)
    noise_levels = values / 1000.0
    l_gtw.wait()
    gg[...] = dot(emb, tw_gen[...])
    l_tt.wait()
    l_ct.wait()

    def modulate(i, carry):
        md[i // 3, lax.rem(i, 3)] = dot(emb, tw[i // 3, lax.rem(i, 3)])
        return carry

    lax.fori_loop(0, 6, modulate, 0)
    l_resid.wait()

    for f, (start, width) in zip(front, FRONT):
        at = slice(start, start + width)
        latent = (resid[:, at].astype(F32) + gg[0:1, at] * sum_end(f)).astype(BF16)
        f["ga"][s] = latent
        lat4[r, :, at] = latent
        gather_start(f)
    noise_forward(FAR)
    for d in (1, 2, 3):
        send(lat4.at[r], lat4.at[r], l_ys.at[d], l_yr.at[r], y_dev(d))
    for level in range(2):
        for model in range(2):
            first = lax.broadcasted_iota(jnp.int32, (16, 1280), 0) == 0
            shift = md[model, 0, 1 + level : 2 + level, :]
            sc[level, model, 256:272, :] = jnp.where(first, shift, 0.0).astype(BF16)

    def prepare(f, start, width, b):
        at = slice(start, start + width)
        rows = pl.ds(pl.multiple_of(b * 16, 16), 16)
        lat = f["ga"][b].astype(F32)
        noi = na[b, :, at].astype(F32)
        for level in range(2):
            sl = noise_levels[1 + level : 2 + level, 0:1]
            noisy = ((1.0 - sl) * lat + sl * noi).astype(BF16).astype(F32)
            square = jnp.sum(noisy * noisy, axis=1, keepdims=True)
            square = jnp.broadcast_to(square, (16, 128))
            if start == 0:
                sqc[level, rows, :] = square
            else:
                sqc[level, rows, :] += square
            for model in range(2):
                scale = 1.0 + md[model, 1, 1 + level : 2 + level, at]
                sc[level, model, rows, at] = (noisy * scale).astype(BF16)

    for f, (start, width) in zip(front, FRONT):
        prepare(f, start, width, s)
        for dz in NEAR_FIRST:
            prepare(f, start, width, gather_step(f, dz))
    for dz in range(8):
        got(na.at[ol * 8 + z_of(dz)], n_xr.at[z_of(dz)])
    l_tq.wait()
    l_cq.wait()

    def product_part(level, model, kind, n):
        at = slice(FRONT[n][0], sum(FRONT[n]))
        return dot(sc[level, model, :, at], wq[model, kind, at])

    for n, (f, (start, width)) in enumerate(zip(front, FRONT)):
        for dz in (0,) + NEAR_FIRST:
            prepare(f, start, width, gather_end(f, dz))
        if n == 0:
            for level in range(2):
                pre[level] = product_part(level, oc, 1, 0)
                of[0, level] = product_part(level, c, 1, 0)

    def other_dots(k):
        kind = (k + 1) % 3
        for level in range(2):
            if k == 0:
                cs[k, level] = (pre[level] + product_part(level, oc, 1, 1)).astype(BF16)
            else:
                cs[k, level] = dot(sc[level, oc], wq[oc, kind]).astype(BF16)
            send(cs.at[k, level], cr.at[k, level], c_s.at[k, level], c_r.at[k, level], core_dev)

    def own_dots(k):
        kind = (k + 1) % 3
        for level in range(2):
            if k == 0:
                of[k, level] += product_part(level, c, 1, 1)
            else:
                of[k % 2, level] = dot(sc[level, c], wq[c, kind])

    def qkv_dots(k):
        other_dots(k)
        own_dots(k)

    def qkv_sums(k):
        for level in range(2):
            got(cr.at[k, level], c_r.at[k, level])
            xs[k, level] = (of[k % 2, level] + cr[k, level].astype(F32)).astype(BF16)
            send(xs.at[k, level], xr.at[k, xh], x_s.at[k, level], x_r.at[k, xh], side_dev(level))

    def square_send():
        for level in range(2):
            sqs[level] = jnp.transpose(sqc[level])[0:8, :]
        send(sqs, cqr, q_s.at[0], q_r.at[0], core_dev)

    def square_pass():
        got(cqr, q_r.at[0])
        sqx[...] = sqs[...] + cqr[...]
        for level in range(2):
            send(sqx.at[level], xqr.at[xh], q_s.at[1 + level], q_r.at[1 + xh], side_dev(level))

    qkv_dots(0)
    square_send()
    other_dots(1)
    qkv_sums(0)
    own_dots(1)
    square_pass()
    other_dots(2)
    qkv_sums(1)
    own_dots(2)
    qkv_sums(2)

    for i in range(2):
        got(xqr.at[i], q_r.at[1 + i])
    square = jnp.broadcast_to((xqr[0] + xqr[1])[0:1, :], (128, 256))
    rinv = lax.rsqrt(jnp.transpose(square) * (1.0 / D) + 1e-06)
    for i in range(2):
        got(nrm.at[i], m_r.at[i])

    def mixed_head(k, h):
        both = xr[k, 0, :, cols(h)].astype(F32) + xr[k, 1, :, cols(h)].astype(F32)
        return both[0:256] * rinv + both[256:257]

    def normed(values, gains):
        factor = lax.rsqrt(jnp.mean(values * values, axis=-1, keepdims=True) + 1e-06)
        return (values * factor * gains).astype(BF16)

    for k in range(2):
        for i in range(2):
            got(xr.at[k, i], x_r.at[k, i])
        for h in range(2):
            values = mixed_head(k, h)
            if k == 0:
                values = normed(values, nrm[c, 1:2, cols(h)])
            kvb[k, r, :, cols(h)] = values.astype(BF16)
        for d in (1, 3):
            send(kvb.at[k, r], kvb.at[k, r], kv_s.at[k, d], kv_r.at[k, r], y_dev(d))
    got(kvb.at[0, below], kv_r.at[0, below])
    send(kvb.at[0, below], kvb.at[0, below], kv_s.at[0, 2], kv_r.at[0, below], y_dev(1))
    for i in range(2):
        got(xr.at[2, i], x_r.at[2, i])
    for h in range(2):
        qb[h] = normed(mixed_head(2, h), nrm[c, 0:1, cols(h)])
    got(kvb.at[1, above], kv_r.at[1, above])
    send(kvb.at[1, above], kvb.at[1, above], kv_s.at[1, 2], kv_r.at[1, above], y_dev(3))
    got(kvb.at[0, above], kv_r.at[0, above])

    exponent = math.log2(math.e) / math.sqrt(HEAD_DIM)
    sums = [jnp.zeros((256, 1), F32)] * 2
    outs = [jnp.zeros((256, 128), F32)] * 2
    for n, b in enumerate((r, above, below, across)):
        if n == 2:
            got(kvb.at[1, below], kv_r.at[1, below])
        if n == 3:
            got(kvb.at[0, across], kv_r.at[0, across])
            got(kvb.at[1, across], kv_r.at[1, across])
        for h in range(2):
            e = jnp.exp2(dot_t(qb[h], kvb[0, b, :, cols(h)]) * exponent)
            sums[h] = sums[h] + jnp.sum(e, axis=1, keepdims=True)
            outs[h] = outs[h] + dot(e.astype(BF16), kvb[1, b, :, cols(h)])
            if n == 3:
                hos[h] = (outs[h] / sums[h]).astype(BF16)
                for level in range(2):
                    send(hos.at[h], ha.at[xh, c, h], h_s.at[level, h], h_r.at[xh, c, h], side_dev(level))

    l_to.wait()
    l_co.wait()

    def out_term(level, model, half):
        rows = pl.ds(pl.multiple_of(half * 128, 128), 128)
        both = jnp.concatenate([ha[level, model, h, rows] for h in range(2)], axis=1)
        sign = (model.astype(F32) - 0.5) * md[model, 2, 1 + level : 2 + level, :]
        return sign * dot(both, ow[model])

    for h in range(2):
        for level in range(2):
            block = ha.at[level, c, h]
            got(block, h_r.at[level, c, h])
            send(block, block, h_s.at[2 + level, h], h_r.at[level, c, h], core_dev)
    for half in range(2):
        acc[half] = out_term(0, c, half) + out_term(1, c, half)
    for h in range(2):
        for level in range(2):
            got(ha.at[level, oc, h], h_r.at[level, oc, h])

    def by_chunk(part, name):
        for f, tiles in zip(tail, TAIL):
            for i, tile in enumerate(tiles):
                piece = part[:, cols(tile)].reshape(8, 16, 128)
                f[name][:, :, cols(i)] = piece.astype(f[name].dtype)

    by_chunk(acc[ol] + out_term(0, oc, ol) + out_term(1, oc, ol), "pb")
    for f in tail:
        sum_start(f)
    by_chunk(acc[xl] + out_term(0, oc, xl) + out_term(1, oc, xl), "pf")
    for f in tail:
        sum_middle(f)
    for d in (1, 2, 3):
        got(lat4.at[y_of(d)], l_yr.at[y_of(d)])
    latent_out[...] = lat4[...].reshape(64, 1280)

    def finish(n):
        f, tiles = tail[n], TAIL[n]
        total = sum_end(f)
        for i, tile in enumerate(tiles):
            f["grad"][i] = (gg[0:1, cols(tile)] * total[:, cols(i)]).astype(BF16)
        if n < 2:
            for d in (2, 1, 3):
                send(f["grad"].at[y_of(d)], f["ga"].at[s, r], f["y_s"].at[d], f["y_r"].at[r], y_dev(d))
            f["ga"][s, r] = f["grad"][r]
        else:
            send(f["grad"].at[1 - odd], f["ga"].at[s, odd], f["y_s"].at[0], f["y_r"].at[odd], pair_dev)
            f["ga"][s, odd] = f["grad"][odd]

    def collect(n):
        f = tail[n]
        if n < 2:
            for d in (1, 3, 2):
                got(f["ga"].at[s, y_of(d)], f["y_r"].at[y_of(d)])
        else:
            got(f["ga"].at[s, 1 - odd], f["y_r"].at[1 - odd])
        gather_start(f)

    def grad_term(n, half):
        at = pl.ds(half * 8, 8)
        lhs = heads[at] if n < 2 else heads[at, pl.ds(2 * pair, 2)]
        rows = 512 if n < 2 else 256
        return lax.dot_general(
            lhs.reshape(rows, 256), tail[n]["ga"][at].reshape(rows, 128),
            (((0,), (0,)), ((), ())), preferred_element_type=F32,
        )

    def product(n):
        f = tail[n]
        half = grad_term(n, xl)
        for dz in range(8):
            gather_end(f, dz)
        f["wg"][r] = (half + grad_term(n, ol)).astype(BF16)
        for d in (2, 1, 3):
            send(f["wg"].at[r], f["wg"].at[r], f["w_s"].at[d], f["w_r"].at[r], y_dev(d))

    def arrived(n):
        f = tail[n]
        for b in (below, above, across):
            got(f["wg"].at[b], f["w_r"].at[b])

    finish(0)
    collect(0)
    finish(1)
    for dz in NEAR_FIRST[:3]:
        gather_step(tail[0], dz)
    collect(1)
    finish(2)
    for dz in NEAR_FIRST[3:]:
        gather_step(tail[0], dz)
    collect(2)
    l_all.wait()
    for dz in NEAR_FIRST:
        gather_step(tail[1], dz)
    product(0)
    for dz in NEAR_FIRST:
        gather_step(tail[2], dz)
    product(1)
    product(2)
    arrived(0)
    arrived(1)
    for n in range(2):
        for i, tile in enumerate(TAIL[n]):
            grad_out[:, cols(tile)] = tail[n]["wg"][i]
    arrived(2)
    for i, tile in enumerate(TAIL[2]):
        both = tail[2]["wg"][i].astype(F32) + tail[2]["wg"][i + 2].astype(F32)
        grad_out[:, cols(tile)] = both.astype(BF16)
    for copy in sent:
        copy.wait_send()


def hand_over(latent, weight_grad, latent_out, grad_out, la, wg, sem):
    pieces = [(latent, la, latent_out)]
    for i in range(2):
        rows = pl.ds(i * 128, 128)
        pieces.append((weight_grad.at[rows], wg.at[rows], grad_out.at[rows]))
    copies = [
        (pltpu.make_async_copy(src, mid, sem.at[0, i]), pltpu.make_async_copy(mid, dst, sem.at[1, i]))
        for i, (src, mid, dst) in enumerate(pieces)
    ]
    for into, _ in copies:
        into.start()
    for into, out in copies:
        into.wait()
        out.start()
    for _, out in copies:
        out.wait()


def on_device(
    gen_heads,
    gen_resid,
    gen_out_w,
    gen_time_w,
    noise,
    steps,
    teacher_qkv,
    teacher_out,
    teacher_time,
    teacher_norm,
    critic_qkv,
    critic_out,
    critic_time,
    critic_norm,
):
    vmem = pl.BlockSpec(memory_space=pltpu.VMEM)
    hbm = pl.BlockSpec(memory_space=pl.ANY)
    V = pltpu.VMEM
    S = pltpu.SemaphoreType.DMA
    block = (16, 1280)
    sums = lambda width: {
        "pb": V((8, 16, width), BF16), "pf": V((8, 16, width), F32),
        "xr": V((8, 16, width), BF16), "zs": V((8, 16, width), BF16), "zr": V((8, 16, width), BF16),
        "xs_s": S((8,)), "xs_r": S((8,)), "zs_s": S((8,)), "zs_r": S((8,)),
        "gz_s": S((8,)), "gz_r": S((8,)), "gx_s": S((8,)), "gx_r": S((8,)),
    }
    front = [{**sums(width), "ga": V((16, 16, width), BF16)} for _, width in FRONT]
    tail = [
        {
            **sums(128 * len(tiles)),
            "grad": V((len(tiles), 16, 128), BF16),
            "ga": V((16, len(tiles), 16, 128), BF16),
            "wg": V((4, 256, 128), BF16),
            "y_s": S((4,)), "y_r": S((4,)), "w_s": S((4,)), "w_r": S((4,)),
        }
        for tiles in TAIL
    ]
    scratch = [
        V((16, 16, 256), BF16), V((16, 4, 16, 256), BF16), V((256, 1280), BF16),
        V((256, 1280), BF16), V(block, BF16), V((2, 3, 1280, 256), BF16),
        V((2, 256, 1280), BF16), V((2, 3, 256, 1280), BF16), V((2, 2, 256), F32),
        V((8, 1280), F32), V((2, 3, 8, 1280), F32),
        V((16,) + block, BF16), V((4,) + block, BF16),
        V((2, 2, 272, 1280), BF16), V((2, 256, 128), F32),
        V((2, 8, 256), F32), V((2, 8, 256), F32), V((2, 8, 256), F32), V((2, 8, 256), F32),
        V((3, 2, 272, 256), BF16), V((3, 2, 272, 256), BF16), V((2, 2, 272, 256), F32), V((2, 272, 256), F32),
        V((3, 2, 272, 256), BF16), V((3, 2, 272, 256), BF16),
        V((2, 4, 256, 256), BF16), V((2, 256, 128), BF16), V((2, 256, 128), BF16),
        V((2, 2, 2, 256, 128), BF16), V((2, 128, 1280), F32),
        front, tail,
        S((12,)), S((8,)), S((8,)), S((8,)), S((8,)), S((4,)), S((4,)),
        S((2,)), S((2,)), S((3,)), S((3,)), S((3, 2)), S((3, 2)), S((3, 2)), S((3, 2)),
        S((2, 4)), S((2, 4)), S((4, 2)), S((2, 2, 2)),
    ]
    latent, weight_grad = pl.pallas_call(
        kernel,
        out_shape=(
            jax.ShapeDtypeStruct((64, 1280), BF16),
            jax.ShapeDtypeStruct((256, 1280), BF16),
        ),
        in_specs=[hbm] * 5 + [pl.BlockSpec(memory_space=pltpu.SMEM)] + [hbm] * 6 + [vmem] * 2,
        out_specs=(vmem, vmem),
        scratch_shapes=scratch,
        compiler_params=pltpu.CompilerParams(
            collective_id=0, has_side_effects=True, vmem_limit_bytes=60 * 1024 * 1024
        ),
        name="step",
    )(
        gen_heads.reshape(16, 4, 16, 256),
        gen_resid.reshape(4, 16, 1280),
        gen_out_w,
        gen_time_w,
        noise.reshape(4, 16, 1280),
        steps,
        teacher_qkv.transpose(1, 0, 2),
        critic_qkv.transpose(1, 0, 2),
        teacher_out,
        critic_out,
        teacher_time.transpose(1, 0, 2),
        critic_time.transpose(1, 0, 2),
        teacher_norm,
        critic_norm,
    )
    return pl.pallas_call(
        hand_over,
        out_shape=(
            jax.ShapeDtypeStruct((64, 1280), BF16),
            jax.ShapeDtypeStruct((256, 1280), BF16),
        ),
        in_specs=[hbm, hbm],
        out_specs=(hbm, hbm),
        scratch_shapes=[V((64, 1280), BF16), V((256, 1280), BF16), S((2, 3))],
        compiler_params=pltpu.CompilerParams(vmem_limit_bytes=60 * 1024 * 1024),
        name="hand_over",
    )(latent, weight_grad)


def solution(mesh):
    in_specs = (
        P(None, "seq"),
        P("seq", "mp"),
        P("seq", "mp"),
        P(None, "mp"),
        P("seq", "mp"),
        P(),
        P("mp", None, "seq"),
        P("seq", "mp"),
        P(None, None, "mp"),
        P(None, "seq"),
        P("mp", None, "seq"),
        P("seq", "mp"),
        P(None, None, "mp"),
        P(None, "seq"),
    )
    out_specs = (P("seq", "mp"), P("seq", "mp"))
    return jax.shard_map(
        on_device, mesh=mesh, in_specs=in_specs, out_specs=out_specs, check_vma=False
    )
```

```python
import math

import jax
import jax.numpy as jnp
from jax import lax
from jax.experimental import pallas as pl
from jax.experimental.pallas import tpu as pltpu
from jax.sharding import PartitionSpec as P

D = 5120
HEAD_DIM = 128
BF16 = jnp.bfloat16
F32 = jnp.float32
MESH = pl.DeviceIdType.MESH
FAR_FIRST = (4, 3, 5, 2, 6, 1, 7)
NEAR_FIRST = (1, 7, 2, 6, 3, 5, 4)


def time_embeds(steps):
    row = lax.broadcasted_iota(jnp.int32, (8, 128), 0)
    values = jnp.where(row == 0, steps[0], jnp.where(row == 1, steps[1], steps[2])).astype(F32)
    positions = lax.broadcasted_iota(jnp.int32, (8, 128), 1).astype(F32)
    angles = values * jnp.exp(positions * (-math.log(10000.0) / 128))
    return jnp.concatenate([jnp.cos(angles), jnp.sin(angles)], axis=1).astype(BF16), values


def dot(a, b):
    return jnp.dot(a, b, preferred_element_type=F32)


def dot_t(a, b):
    return lax.dot_general(a, b, (((1,), (1,)), ((), ())), preferred_element_type=F32)


FRONT = ((0, 768), (768, 512))
NEAR, FAR = NEAR_FIRST[:4], NEAR_FIRST[4:]
TAIL = ((0, 3, 6, 8), (1, 4, 7, 9), (2, 5))


def cols(i, n=1):
    return slice(i * 128, (i + n) * 128)


def kernel(
    gh4, resid4, gow, gtw, noise4, steps, tq, cq, tow, cow, ttw, ctw, t_norm, c_norm,
    latent_out, grad_out,
    heads_r, heads, ow_gen, tw_gen, resid, wq, ow, tw, nrm, gg, md,
    na, lat4, sc, sqc, sqs, cqr, sqx, xqr,
    cs, cr, of, pre, xs, xr, kvb, qb, hos, ha, acc,
    front, tail,
    lsem, n_zs, n_zr, n_xs, n_xr, l_ys, l_yr,
    m_s, m_r, q_s, q_r, c_s, c_r, x_s, x_r, kv_s, kv_r, h_s, h_r,
):
    r = lax.axis_index("role")
    s = lax.axis_index("seq")
    m = lax.axis_index("mp")
    xl, z = s // 8, lax.rem(s, 8)
    xh, c = m // 2, lax.rem(m, 2)
    ol = 1 - xl
    oc = 1 - c
    z_of = lambda dz: lax.rem(z + dz, 8)
    z_dev = lambda dz: {"seq": xl * 8 + z_of(dz)}
    x_dev = {"seq": ol * 8 + z}
    core_dev = {"mp": 2 * xh + oc}
    side_dev = lambda level: {"seq": ol * 8 + z, "mp": 2 * level + c}
    y_of = lambda d: lax.rem(r + d, 4)
    y_dev = lambda d: {"role": y_of(d)}
    below, above, across = y_of(3), y_of(1), y_of(2)
    pair, odd = r // 2, lax.rem(r, 2)
    pair_dev = {"role": 2 * pair + 1 - odd}

    def rc(src, dst, ssem, rsem, dev):
        return pltpu.make_async_remote_copy(
            src_ref=src, dst_ref=dst, send_sem=ssem, recv_sem=rsem,
            device_id=dev, device_id_type=MESH,
        )

    sent = []

    def send(*args):
        copy = rc(*args)
        copy.start()
        sent.append(copy)

    def got(dst, rsem):
        rc(dst, dst, rsem, rsem, x_dev).wait_recv()

    loads = []

    def load(src, dst):
        copy = pltpu.make_async_copy(src, dst, lsem.at[len(loads)])
        copy.start()
        loads.append(copy)
        return copy

    barrier = pltpu.get_barrier_semaphore()
    peers = [z_dev(dz) for dz in range(1, 8)] + [x_dev, core_dev]
    peers += [side_dev(1 - xh)] + [y_dev(d) for d in (1, 2, 3)]
    for dev in peers:
        pl.semaphore_signal(barrier, inc=1, device_id=dev, device_id_type=MESH)
    l_heads = load(gh4.at[:, r], heads_r)
    l_gow = load(gow, ow_gen)
    l_noise = load(noise4.at[r], na.at[s])
    l_resid = load(resid4.at[r], resid)
    l_gtw = load(gtw, tw_gen)
    l_tt = load(ttw, tw.at[0])
    l_ct = load(ctw, tw.at[1])
    l_tq = load(tq, wq.at[0])
    l_cq = load(cq, wq.at[1])
    l_to = load(tow, ow.at[0])
    l_co = load(cow, ow.at[1])
    l_all = load(gh4, heads)
    l_heads.wait()
    l_gow.wait()
    l_noise.wait()

    def first_part(n):
        start, width = FRONT[n]
        part = dot(heads_r[pl.ds(ol * 8, 8)].reshape(128, 256), ow_gen[:, start : start + width])
        front[n]["pb"][...] = part.astype(BF16).reshape(8, 16, width)

    first_part(0)
    pl.semaphore_wait(barrier, len(peers))

    def sum_start(f):
        for dz in FAR_FIRST + (0,):
            zz = z_of(dz)
            send(f["pb"].at[zz], f["xr"].at[zz], f["xs_s"].at[zz], f["xs_r"].at[zz], x_dev)

    def sum_middle(f):
        for dz in FAR_FIRST:
            zz = z_of(dz)
            got(f["xr"].at[zz], f["xs_r"].at[zz])
            f["zs"][zz] = (f["pf"][zz] + f["xr"][zz].astype(F32)).astype(BF16)
            send(f["zs"].at[zz], f["zr"].at[z], f["zs_s"].at[dz], f["zs_r"].at[z], z_dev(dz))

    def sum_end(f):
        got(f["xr"].at[z], f["xs_r"].at[z])
        total = f["pf"][z] + f["xr"][z].astype(F32)
        for dz in NEAR_FIRST:
            zz = z_of(dz)
            got(f["zr"].at[zz], f["zs_r"].at[zz])
            total = total + f["zr"][zz].astype(F32)
        return total

    def gather_start(f):
        own = f["ga"].at[s]
        for dz in NEAR_FIRST:
            send(own, own, f["gz_s"].at[dz], f["gz_r"].at[z], z_dev(dz))
        send(own, own, f["gx_s"].at[z], f["gx_r"].at[z], x_dev)

    def gather_step(f, dz):
        zz = z_of(dz)
        block = f["ga"].at[xl * 8 + zz]
        got(block, f["gz_r"].at[zz])
        send(block, block, f["gx_s"].at[zz], f["gx_r"].at[zz], x_dev)
        return xl * 8 + zz

    def gather_end(f, dz):
        zz = z_of(dz)
        got(f["ga"].at[ol * 8 + zz], f["gx_r"].at[zz])
        return ol * 8 + zz

    def noise_start(distances):
        for dz in distances:
            send(na.at[s], na.at[s], n_zs.at[dz], n_zr.at[z], z_dev(dz))

    def noise_forward(distances):
        for dz in distances:
            zz = z_of(dz)
            got(na.at[xl * 8 + zz], n_zr.at[zz])
            send(na.at[xl * 8 + zz], na.at[xl * 8 + zz], n_xs.at[zz], n_xr.at[zz], x_dev)

    noise_start(NEAR)
    sum_start(front[0])
    first_part(1)
    sum_start(front[1])
    for i, norm in enumerate((t_norm, c_norm)):
        send(norm, nrm.at[i], m_s.at[i], m_r.at[i], x_dev)
    send(na.at[s], na.at[s], n_xs.at[z], n_xr.at[z], x_dev)
    part = dot(heads_r[pl.ds(xl * 8, 8)].reshape(128, 256), ow_gen[...])
    for f, (start, width) in zip(front, FRONT):
        f["pf"][...] = part[:, start : start + width].reshape(8, 16, width)
    for f in front:
        sum_middle(f)
    noise_start(FAR)
    noise_forward(NEAR)

    emb, values = time_embeds(steps)
    noise_levels = values / 1000.0
    l_gtw.wait()
    gg[...] = dot(emb, tw_gen[...])
    l_tt.wait()
    l_ct.wait()

    def modulate(i, carry):
        md[i // 3, lax.rem(i, 3)] = dot(emb, tw[i // 3, lax.rem(i, 3)])
        return carry

    lax.fori_loop(0, 6, modulate, 0)
    l_resid.wait()

    for f, (start, width) in zip(front, FRONT):
        at = slice(start, start + width)
        latent = (resid[:, at].astype(F32) + gg[0:1, at] * sum_end(f)).astype(BF16)
        f["ga"][s] = latent
        lat4[r, :, at] = latent
        gather_start(f)
    noise_forward(FAR)
    for d in (1, 2, 3):
        send(lat4.at[r], lat4.at[r], l_ys.at[d], l_yr.at[r], y_dev(d))
    for level in range(2):
        for model in range(2):
            first = lax.broadcasted_iota(jnp.int32, (16, 1280), 0) == 0
            shift = md[model, 0, 1 + level : 2 + level, :]
            sc[level, model, 256:272, :] = jnp.where(first, shift, 0.0).astype(BF16)

    def prepare(f, start, width, b):
        at = slice(start, start + width)
        rows = pl.ds(pl.multiple_of(b * 16, 16), 16)
        lat = f["ga"][b].astype(F32)
        noi = na[b, :, at].astype(F32)
        for level in range(2):
            sl = noise_levels[1 + level : 2 + level, 0:1]
            noisy = ((1.0 - sl) * lat + sl * noi).astype(BF16).astype(F32)
            square = jnp.sum(noisy * noisy, axis=1, keepdims=True)
            square = jnp.broadcast_to(square, (16, 128))
            if start == 0:
                sqc[level, rows, :] = square
            else:
                sqc[level, rows, :] += square
            for model in range(2):
                scale = 1.0 + md[model, 1, 1 + level : 2 + level, at]
                sc[level, model, rows, at] = (noisy * scale).astype(BF16)

    for f, (start, width) in zip(front, FRONT):
        prepare(f, start, width, s)
        for dz in NEAR_FIRST:
            prepare(f, start, width, gather_step(f, dz))
    for dz in range(8):
        got(na.at[ol * 8 + z_of(dz)], n_xr.at[z_of(dz)])
    l_tq.wait()
    l_cq.wait()

    def product_part(level, model, kind, n):
        at = slice(FRONT[n][0], sum(FRONT[n]))
        return dot(sc[level, model, :, at], wq[model, kind, at])

    for n, (f, (start, width)) in enumerate(zip(front, FRONT)):
        for dz in (0,) + NEAR_FIRST:
            prepare(f, start, width, gather_end(f, dz))
        if n == 0:
            for level in range(2):
                pre[level] = product_part(level, oc, 1, 0)
                of[0, level] = product_part(level, c, 1, 0)

    def other_dots(k):
        kind = (k + 1) % 3
        for level in range(2):
            if k == 0:
                cs[k, level] = (pre[level] + product_part(level, oc, 1, 1)).astype(BF16)
            else:
                cs[k, level] = dot(sc[level, oc], wq[oc, kind]).astype(BF16)
            send(cs.at[k, level], cr.at[k, level], c_s.at[k, level], c_r.at[k, level], core_dev)

    def own_dots(k):
        kind = (k + 1) % 3
        for level in range(2):
            if k == 0:
                of[k, level] += product_part(level, c, 1, 1)
            else:
                of[k % 2, level] = dot(sc[level, c], wq[c, kind])

    def qkv_dots(k):
        other_dots(k)
        own_dots(k)

    def qkv_sums(k):
        for level in range(2):
            got(cr.at[k, level], c_r.at[k, level])
            xs[k, level] = (of[k % 2, level] + cr[k, level].astype(F32)).astype(BF16)
            send(xs.at[k, level], xr.at[k, xh], x_s.at[k, level], x_r.at[k, xh], side_dev(level))

    def square_send():
        for level in range(2):
            sqs[level] = jnp.transpose(sqc[level])[0:8, :]
        send(sqs, cqr, q_s.at[0], q_r.at[0], core_dev)

    def square_pass():
        got(cqr, q_r.at[0])
        sqx[...] = sqs[...] + cqr[...]
        for level in range(2):
            send(sqx.at[level], xqr.at[xh], q_s.at[1 + level], q_r.at[1 + xh], side_dev(level))

    qkv_dots(0)
    square_send()
    other_dots(1)
    qkv_sums(0)
    own_dots(1)
    square_pass()
    other_dots(2)
    qkv_sums(1)
    own_dots(2)
    qkv_sums(2)

    for i in range(2):
        got(xqr.at[i], q_r.at[1 + i])
    square = jnp.broadcast_to((xqr[0] + xqr[1])[0:1, :], (128, 256))
    rinv = lax.rsqrt(jnp.transpose(square) * (1.0 / D) + 1e-06)
    for i in range(2):
        got(nrm.at[i], m_r.at[i])

    def mixed_head(k, h):
        both = xr[k, 0, :, cols(h)].astype(F32) + xr[k, 1, :, cols(h)].astype(F32)
        return both[0:256] * rinv + both[256:257]

    def normed(values, gains):
        factor = lax.rsqrt(jnp.mean(values * values, axis=-1, keepdims=True) + 1e-06)
        return (values * factor * gains).astype(BF16)

    for k in range(2):
        for i in range(2):
            got(xr.at[k, i], x_r.at[k, i])
        for h in range(2):
            values = mixed_head(k, h)
            if k == 0:
                values = normed(values, nrm[c, 1:2, cols(h)])
            kvb[k, r, :, cols(h)] = values.astype(BF16)
        for d in (1, 3):
            send(kvb.at[k, r], kvb.at[k, r], kv_s.at[k, d], kv_r.at[k, r], y_dev(d))
    got(kvb.at[0, below], kv_r.at[0, below])
    send(kvb.at[0, below], kvb.at[0, below], kv_s.at[0, 2], kv_r.at[0, below], y_dev(1))
    for i in range(2):
        got(xr.at[2, i], x_r.at[2, i])
    for h in range(2):
        qb[h] = normed(mixed_head(2, h), nrm[c, 0:1, cols(h)])
    got(kvb.at[1, above], kv_r.at[1, above])
    send(kvb.at[1, above], kvb.at[1, above], kv_s.at[1, 2], kv_r.at[1, above], y_dev(3))
    got(kvb.at[0, above], kv_r.at[0, above])

    exponent = math.log2(math.e) / math.sqrt(HEAD_DIM)
    sums = [jnp.zeros((256, 1), F32)] * 2
    outs = [jnp.zeros((256, 128), F32)] * 2
    for n, b in enumerate((r, above, below, across)):
        if n == 2:
            got(kvb.at[1, below], kv_r.at[1, below])
        if n == 3:
            got(kvb.at[0, across], kv_r.at[0, across])
            got(kvb.at[1, across], kv_r.at[1, across])
        for h in range(2):
            e = jnp.exp2(dot_t(qb[h], kvb[0, b, :, cols(h)]) * exponent)
            sums[h] = sums[h] + jnp.sum(e, axis=1, keepdims=True)
            outs[h] = outs[h] + dot(e.astype(BF16), kvb[1, b, :, cols(h)])
            if n == 3:
                hos[h] = (outs[h] / sums[h]).astype(BF16)
                for level in range(2):
                    send(hos.at[h], ha.at[xh, c, h], h_s.at[level, h], h_r.at[xh, c, h], side_dev(level))

    l_to.wait()
    l_co.wait()

    def out_term(level, model, half):
        rows = pl.ds(pl.multiple_of(half * 128, 128), 128)
        both = jnp.concatenate([ha[level, model, h, rows] for h in range(2)], axis=1)
        sign = (model.astype(F32) - 0.5) * md[model, 2, 1 + level : 2 + level, :]
        return sign * dot(both, ow[model])

    for h in range(2):
        for level in range(2):
            block = ha.at[level, c, h]
            got(block, h_r.at[level, c, h])
            send(block, block, h_s.at[2 + level, h], h_r.at[level, c, h], core_dev)
    for half in range(2):
        acc[half] = out_term(0, c, half) + out_term(1, c, half)
    for h in range(2):
        for level in range(2):
            got(ha.at[level, oc, h], h_r.at[level, oc, h])

    def by_chunk(part, name, start=False):
        for f, tiles in zip(tail, TAIL):
            for i, tile in enumerate(tiles):
                piece = part[:, cols(tile)].reshape(8, 16, 128)
                f[name][:, :, cols(i)] = piece.astype(f[name].dtype)
            if start:
                sum_start(f)

    by_chunk(acc[ol] + out_term(0, oc, ol) + out_term(1, oc, ol), "pb", True)
    by_chunk(acc[xl] + out_term(0, oc, xl) + out_term(1, oc, xl), "pf")
    for f in tail:
        sum_middle(f)
    for d in (1, 2, 3):
        got(lat4.at[y_of(d)], l_yr.at[y_of(d)])
    latent_out[...] = lat4[...].reshape(64, 1280)

    def finish(n):
        f, tiles = tail[n], TAIL[n]
        total = sum_end(f)
        for i, tile in enumerate(tiles):
            f["grad"][i] = (gg[0:1, cols(tile)] * total[:, cols(i)]).astype(BF16)
        if n < 2:
            for d in (2, 1, 3):
                send(f["grad"].at[y_of(d)], f["ga"].at[s, r], f["y_s"].at[d], f["y_r"].at[r], y_dev(d))
            f["ga"][s, r] = f["grad"][r]
        else:
            send(f["grad"].at[1 - odd], f["ga"].at[s, odd], f["y_s"].at[0], f["y_r"].at[odd], pair_dev)
            f["ga"][s, odd] = f["grad"][odd]

    def collect(n):
        f = tail[n]
        if n < 2:
            for d in (1, 3, 2):
                got(f["ga"].at[s, y_of(d)], f["y_r"].at[y_of(d)])
        else:
            got(f["ga"].at[s, 1 - odd], f["y_r"].at[1 - odd])
        gather_start(f)

    def grad_term(n, half):
        at = pl.ds(half * 8, 8)
        lhs = heads[at] if n < 2 else heads[at, pl.ds(2 * pair, 2)]
        rows = 512 if n < 2 else 256
        return lax.dot_general(
            lhs.reshape(rows, 256), tail[n]["ga"][at].reshape(rows, 128),
            (((0,), (0,)), ((), ())), preferred_element_type=F32,
        )

    def product(n):
        f = tail[n]
        half = grad_term(n, xl)
        for dz in range(8):
            gather_end(f, dz)
        f["wg"][r] = (half + grad_term(n, ol)).astype(BF16)
        for d in (2, 1, 3):
            send(f["wg"].at[r], f["wg"].at[r], f["w_s"].at[d], f["w_r"].at[r], y_dev(d))

    def arrived(n):
        f = tail[n]
        for b in (below, above, across):
            got(f["wg"].at[b], f["w_r"].at[b])

    finish(0)
    collect(0)
    finish(1)
    for dz in NEAR_FIRST[:3]:
        gather_step(tail[0], dz)
    collect(1)
    finish(2)
    for dz in NEAR_FIRST[3:]:
        gather_step(tail[0], dz)
    collect(2)
    l_all.wait()
    for dz in NEAR_FIRST:
        gather_step(tail[1], dz)
    product(0)
    for dz in NEAR_FIRST:
        gather_step(tail[2], dz)
    product(1)
    product(2)
    arrived(0)
    arrived(1)
    for n in range(2):
        for i, tile in enumerate(TAIL[n]):
            grad_out[:, cols(tile)] = tail[n]["wg"][i]
    arrived(2)
    for i, tile in enumerate(TAIL[2]):
        both = tail[2]["wg"][i].astype(F32) + tail[2]["wg"][i + 2].astype(F32)
        grad_out[:, cols(tile)] = both.astype(BF16)
    for copy in sent:
        copy.wait_send()


def hand_over(latent, weight_grad, latent_out, grad_out, la, wg, sem):
    pieces = [(latent, la, latent_out)]
    for i in range(2):
        rows = pl.ds(i * 128, 128)
        pieces.append((weight_grad.at[rows], wg.at[rows], grad_out.at[rows]))
    copies = [
        (pltpu.make_async_copy(src, mid, sem.at[0, i]), pltpu.make_async_copy(mid, dst, sem.at[1, i]))
        for i, (src, mid, dst) in enumerate(pieces)
    ]
    for into, _ in copies:
        into.start()
    for into, out in copies:
        into.wait()
        out.start()
    for _, out in copies:
        out.wait()


def on_device(
    gen_heads,
    gen_resid,
    gen_out_w,
    gen_time_w,
    noise,
    steps,
    teacher_qkv,
    teacher_out,
    teacher_time,
    teacher_norm,
    critic_qkv,
    critic_out,
    critic_time,
    critic_norm,
):
    vmem = pl.BlockSpec(memory_space=pltpu.VMEM)
    hbm = pl.BlockSpec(memory_space=pl.ANY)
    V = pltpu.VMEM
    S = pltpu.SemaphoreType.DMA
    block = (16, 1280)
    sums = lambda width: {
        "pb": V((8, 16, width), BF16), "pf": V((8, 16, width), F32),
        "xr": V((8, 16, width), BF16), "zs": V((8, 16, width), BF16), "zr": V((8, 16, width), BF16),
        "xs_s": S((8,)), "xs_r": S((8,)), "zs_s": S((8,)), "zs_r": S((8,)),
        "gz_s": S((8,)), "gz_r": S((8,)), "gx_s": S((8,)), "gx_r": S((8,)),
    }
    front = [{**sums(width), "ga": V((16, 16, width), BF16)} for _, width in FRONT]
    tail = [
        {
            **sums(128 * len(tiles)),
            "grad": V((len(tiles), 16, 128), BF16),
            "ga": V((16, len(tiles), 16, 128), BF16),
            "wg": V((4, 256, 128), BF16),
            "y_s": S((4,)), "y_r": S((4,)), "w_s": S((4,)), "w_r": S((4,)),
        }
        for tiles in TAIL
    ]
    scratch = [
        V((16, 16, 256), BF16), V((16, 4, 16, 256), BF16), V((256, 1280), BF16),
        V((256, 1280), BF16), V(block, BF16), V((2, 3, 1280, 256), BF16),
        V((2, 256, 1280), BF16), V((2, 3, 256, 1280), BF16), V((2, 2, 256), F32),
        V((8, 1280), F32), V((2, 3, 8, 1280), F32),
        V((16,) + block, BF16), V((4,) + block, BF16),
        V((2, 2, 272, 1280), BF16), V((2, 256, 128), F32),
        V((2, 8, 256), F32), V((2, 8, 256), F32), V((2, 8, 256), F32), V((2, 8, 256), F32),
        V((3, 2, 272, 256), BF16), V((3, 2, 272, 256), BF16), V((2, 2, 272, 256), F32), V((2, 272, 256), F32),
        V((3, 2, 272, 256), BF16), V((3, 2, 272, 256), BF16),
        V((2, 4, 256, 256), BF16), V((2, 256, 128), BF16), V((2, 256, 128), BF16),
        V((2, 2, 2, 256, 128), BF16), V((2, 128, 1280), F32),
        front, tail,
        S((12,)), S((8,)), S((8,)), S((8,)), S((8,)), S((4,)), S((4,)),
        S((2,)), S((2,)), S((3,)), S((3,)), S((3, 2)), S((3, 2)), S((3, 2)), S((3, 2)),
        S((2, 4)), S((2, 4)), S((4, 2)), S((2, 2, 2)),
    ]
    latent, weight_grad = pl.pallas_call(
        kernel,
        out_shape=(
            jax.ShapeDtypeStruct((64, 1280), BF16),
            jax.ShapeDtypeStruct((256, 1280), BF16),
        ),
        in_specs=[hbm] * 5 + [pl.BlockSpec(memory_space=pltpu.SMEM)] + [hbm] * 6 + [vmem] * 2,
        out_specs=(vmem, vmem),
        scratch_shapes=scratch,
        compiler_params=pltpu.CompilerParams(
            collective_id=0, has_side_effects=True, vmem_limit_bytes=60 * 1024 * 1024
        ),
        name="step",
    )(
        gen_heads.reshape(16, 4, 16, 256),
        gen_resid.reshape(4, 16, 1280),
        gen_out_w,
        gen_time_w,
        noise.reshape(4, 16, 1280),
        steps,
        teacher_qkv.transpose(1, 0, 2),
        critic_qkv.transpose(1, 0, 2),
        teacher_out,
        critic_out,
        teacher_time.transpose(1, 0, 2),
        critic_time.transpose(1, 0, 2),
        teacher_norm,
        critic_norm,
    )
    return pl.pallas_call(
        hand_over,
        out_shape=(
            jax.ShapeDtypeStruct((64, 1280), BF16),
            jax.ShapeDtypeStruct((256, 1280), BF16),
        ),
        in_specs=[hbm, hbm],
        out_specs=(hbm, hbm),
        scratch_shapes=[V((64, 1280), BF16), V((256, 1280), BF16), S((2, 3))],
        compiler_params=pltpu.CompilerParams(vmem_limit_bytes=60 * 1024 * 1024),
        name="hand_over",
    )(latent, weight_grad)


def solution(mesh):
    in_specs = (
        P(None, "seq"),
        P("seq", "mp"),
        P("seq", "mp"),
        P(None, "mp"),
        P("seq", "mp"),
        P(),
        P("mp", None, "seq"),
        P("seq", "mp"),
        P(None, None, "mp"),
        P(None, "seq"),
        P("mp", None, "seq"),
        P("seq", "mp"),
        P(None, None, "mp"),
        P(None, "seq"),
    )
    out_specs = (P("seq", "mp"), P("seq", "mp"))
    return jax.shard_map(
        on_device, mesh=mesh, in_specs=in_specs, out_specs=out_specs, check_vma=False
    )
```
